32 devices in a mesh: groups: 2 (over y), expert: 4 (over z), dp: 4 (over x, core).
Axes of the slice: x: 2, y: 2, z: 4, core: 2. Of those that a mesh axis runs over, the one named last changes fastest.
Arguments:
- tokens: bfloat16 [512, 6144], P(('groups', 'expert'), 'dp'), parts along dimension 0, may hold values from -6 to 6
- expert_ids: int32 [512, 8], P(('groups', 'expert')), parts along dimension 0, may hold values from 0 to 31, all different within a row; in each aligned block of 64 rows (0 to 63, 64 to 127, ...) at most 32 rows name the same one
- scores: float32 [512, 8], P(('groups', 'expert')), parts along dimension 0, may hold values from -8 to 8
- w_gate: bfloat16 [32, 6144, 1024], P('expert', 'dp'), may hold values from -0.078125 to 0.078125
- w_up: bfloat16 [32, 6144, 1024], P('expert', 'dp'), may hold values from -0.078125 to 0.078125
- w_down: bfloat16 [32, 1024, 6144], P('expert', None, 'dp'), may hold values from -0.1875 to 0.1875
Outputs:
- mixed: bfloat16 [512, 6144], P(('groups', 'expert'), 'dp'), parts along dimension 0
The draws below stay inside these ranges and needn't reach their ends.
There are 2 independent parts, one for each index of `groups`. The reference program is written for one: setup_inputs(seed, part) draws one part's arguments, and reference() takes and returns one part's arrays. A program takes and returns all parts, laid end to end along the dimension named above; an argument that names none is the same for every part. Nothing has to cross between parts.
Inputs may be any that keep to these rules, and one draw needn't show every extreme that they name: `expert_ids`: each row names 8 different experts; among the rows of one index of expert (aligned blocks of 64 rows) no expert is named by more than 32 rows, a bound that some block reaches.
All inputs are finite; a program needn't handle non-finite values.
Results may differ from the reference program's by a relative error of at most 0.024.
Values may be sent and summed in bfloat16 or wider, within the bound.
A program may use at most 128 MiB of HBM per device.

```python
import math
import jax
import jax.numpy as jnp
import numpy as np
from jax import lax

D = 6144
H = 1024
EXPERTS = 32
TOP = 8
TOK_DEV = 64
CAP = 32
TOKENS = 256
N_EXPERT = 4
N_DP = 4


def levels(own_key, dims, split, low, top_value):
    factor_of = 1.0
    for position, blocks in split:
        heights = jax.random.uniform(jax.random.fold_in(jax.random.fold_in(own_key, 6), position), (blocks,), jnp.float32, low / len(split), top_value / len(split))
        factor_of = factor_of * jnp.repeat(jnp.exp(heights), dims[position] // blocks).reshape((-1,) + (1,) * (len(dims) - 1 - position))
    return factor_of


def shared_out(rng, own, number, rows, number_of, top, limit, skew):
    order = jax.random.permutation(rng, number_of)
    packed, usual = load_shares(number_of, rows * top, limit, skew, True), load_shares(number_of, rows * top, limit, skew, False)
    places = jnp.arange(number_of)

    def named(tallies, offset_by):
        used = int((tallies > 0).sum())
        fixed = max(1, used // 4)
        moved = fixed + (places - fixed + offset_by * (used - fixed)) % max(1, number_of - fixed)
        return jnp.zeros((number_of,), jnp.int32).at[order[jnp.where(places < fixed, places, moved)]].set(jnp.asarray(tallies, jnp.int32))

    tallies = jnp.where(number % 4 == 0, named(packed, number // 4), named(usual, number - number // 4 - 1))
    mixed = jax.random.permutation(jax.random.fold_in(own, 3), number_of)
    donor, sink = mixed[0:number_of // 2 * 2:2], mixed[1:number_of // 2 * 2:2]
    room = jnp.minimum(tallies[donor] - 1, limit - tallies[sink]) // 2
    room = jnp.where((donor == order[0]) | (sink == order[0]) | (tallies[sink] == 0), 0, jnp.maximum(room, 0))
    moved = jax.random.randint(jax.random.fold_in(own, 4), (number_of // 2,), 0, 1 << 20) % (room + 1)
    tallies = tallies.at[donor].add(-moved).at[sink].add(moved)
    members = jnp.searchsorted(jnp.cumsum(tallies), jnp.arange(rows * top), side="right").astype(jnp.int32)
    grid = members.reshape(top, rows).T
    grid = grid[jax.random.permutation(jax.random.fold_in(own, 1), rows)]
    offset_by = jax.random.randint(jax.random.fold_in(own, 2), (rows, 1), 0, top)
    return jnp.take_along_axis(grid, (jnp.arange(top)[None, :] + offset_by) % top, axis=1)


def load_shares(count, total, limit, slope, full):
    weights = [(1 << 20) // math.isqrt(rank ** slope) + 1 for rank in range(1, count + 1)]
    largest = limit if full else min(limit, max(-(-total // count), total * weights[0] // sum(weights)))
    least = 1 if total - largest >= count - 1 else 0
    counts, spare = [largest] + [least] * (count - 1), total - largest - least * (count - 1)
    while spare > 0:
        movable = [i for i in range(1, count) if counts[i] < largest] or [i for i in range(1, count) if counts[i] < limit]
        whole, remaining = sum([weights[i] for i in movable]), spare
        for i in movable:
            more = min(limit - counts[i], max(1, remaining * weights[i] // whole), spare)
            counts[i] = counts[i] + more
            spare = spare - more
    return np.array(counts)


def bell_draw(stream_key, shape, deviation, most, split=(), kind=jnp.bfloat16):
    result = deviation * jax.random.normal(stream_key, shape, jnp.float32)
    if split:
        result = result * levels(stream_key, shape, split, -0.22, 0.18)
    return jnp.clip(result, -most, most).astype(kind)


def setup_inputs(seed: int = 0, part: int = 0) -> dict:
    keys = jax.random.split(jax.random.key(seed), 7)
    own_keys = jax.random.split(jax.random.fold_in(keys[6], part), 7)
    tokens = bell_draw(own_keys[0], (TOKENS, D), 1.0, 6.0, ((0, 4), (1, 4)))
    expert_ids_keys = jax.random.split(jax.random.fold_in(own_keys[1], 1), TOKENS // TOK_DEV)
    expert_ids_turns = jax.random.permutation(jax.random.fold_in(own_keys[1], 3), TOKENS // TOK_DEV)
    expert_ids = jax.vmap(lambda own, number: shared_out(jax.random.fold_in(own_keys[1], 2), own, number, TOK_DEV, EXPERTS, TOP, CAP, 2))(expert_ids_keys, expert_ids_turns).reshape((TOKENS, TOP))
    scores = bell_draw(own_keys[2], (TOKENS, TOP), 2.0, 8.0, ((0, 4),), jnp.float32)
    w_gate = bell_draw(keys[3], (EXPERTS, D, H), D ** -0.5, 0.078125, ((0, 4), (1, 4)))
    w_up = bell_draw(keys[4], (EXPERTS, D, H), D ** -0.5, 0.078125, ((0, 4), (1, 4)))
    w_down = bell_draw(keys[5], (EXPERTS, H, D), H ** -0.5, 0.1875, ((0, 4), (2, 4)))
    return dict(tokens=tokens, expert_ids=expert_ids, scores=scores, w_gate=w_gate, w_up=w_up, w_down=w_down)


def block_sum(parts, weight):
    local = D // N_DP
    blocks = jnp.einsum('rbd,bdh->rbh', parts, weight.reshape(N_DP, local, H).astype(jnp.float32))
    rounded = lax.optimization_barrier(blocks.astype(jnp.bfloat16))
    return jnp.sum(rounded.astype(jnp.float32), axis=1)


def reference(tokens, expert_ids, scores, w_gate, w_up, w_down):
    n_blocks = N_EXPERT
    ids = expert_ids.reshape(n_blocks, TOK_DEV * TOP)
    onehot = (ids[:, :, None] == jnp.arange(EXPERTS, dtype=jnp.int32)[None, None, :]).astype(jnp.int32)
    earlier = jnp.cumsum(onehot, axis=1) - onehot
    rank = jnp.sum(earlier * onehot, axis=2)
    block = jnp.arange(n_blocks, dtype=jnp.int32)[:, None]
    slots = ((ids * n_blocks + block) * CAP + rank).reshape(-1).astype(jnp.int32)
    source = jnp.repeat(jnp.arange(TOKENS, dtype=jnp.int32), TOP)
    buffer = jnp.zeros((EXPERTS * n_blocks * CAP, D), jnp.bfloat16).at[slots].set(tokens[source])
    buffer = buffer.reshape(EXPERTS, n_blocks * CAP, D)

    def expert_rows(items):
        rows, gate_w, up_w, down_w = items
        parts = rows.reshape(-1, N_DP, D // N_DP).astype(jnp.float32)
        gate = block_sum(parts, gate_w)
        up = block_sum(parts, up_w)
        hidden = (jax.nn.silu(gate) * up).astype(jnp.bfloat16)
        return jnp.dot(hidden, down_w, preferred_element_type=jnp.float32).astype(jnp.bfloat16)

    outputs = lax.map(expert_rows, (buffer, w_gate, w_up, w_down))
    picked = outputs.reshape(-1, D)[slots].reshape(TOKENS, TOP, D).astype(jnp.float32)
    affinity = jax.nn.sigmoid(scores)
    weights = 2.5 * affinity / jnp.sum(affinity, axis=1, keepdims=True)
    return jnp.einsum('tk,tkd->td', weights, picked).astype(jnp.bfloat16)
```

```python
import functools

import jax
import jax.numpy as jnp
from jax import lax
from jax.experimental import pallas as pl
from jax.experimental.pallas import tpu as pltpu
from jax.sharding import PartitionSpec as P

MESH = pl.DeviceIdType.MESH
F32, BF16 = jnp.float32, jnp.bfloat16
LAGS = (0, 1, 3, 5, 7)
LINE_LAGS = (0, 1, 3, 5, 6)


def dot(a, b, dims=((1,), (0,))):
    return lax.dot_general(a, b, (dims, ((), ())), preferred_element_type=F32)


def remote(src, dst, send, recv, **where):
    return pltpu.make_async_remote_copy(
        src_ref=src, dst_ref=dst, send_sem=send, recv_sem=recv,
        device_id=where, device_id_type=MESH,
    )


def tile_of(size):
    for tile in (512, 384, 256, 128):
        if size % tile == 0:
            return tile
    return size


def kernel(dims, tok_ref, ids_ref, sco_ref, wg_hbm, wu_hbm, wd_hbm, out_ref,
           wg, wu, wd, xall, route, slot_c, wgt_c, rows, s1, r1, keep, s2, r2, hid, acc,
           rs_s, rs_in,
           wsem, dsem, ag_s, ag_r, p_s, p_r, q_s, q_r, h_s, h_r, f_r, t_s, t_r):
    E, DP, EL, NCH, G, CAP, NB, ND, LINE, ct = dims
    M = DP // 2
    tok, width = tok_ref.shape
    top = ids_ref.shape[0]
    H = wg.shape[2]
    hb = H // DP
    R, T = G * CAP, G * tok
    N = EL * NCH
    K = EL // 2
    half = tok // 2
    EP = slot_c.shape[1]
    e = lax.axis_index("expert")
    d = lax.axis_index("dp")
    x, c = lax.div(d, 2), lax.rem(d, 2)
    mate = 2 * x + 1 - c
    has_left, has_right = e > 0, e < E - 1
    if LINE:
        low = e < 2
        mid = (e == 1) | (e == 2)
        onward = jnp.where(low, 0, 1)
        nb = jnp.where(low, e + 1, e - 1)
        fb = jnp.where(low, 3, 0)
        fa = 6 - e - nb - fb
        order = (e, nb, fa, fb)

    def across(k):
        return lax.rem(x + k, M)

    def source(k):
        return lax.rem(x + M - k, M)

    def w_gu(j, slot):
        return (pltpu.make_async_copy(wg_hbm.at[j], wg.at[slot], wsem.at[0, slot]),
                pltpu.make_async_copy(wu_hbm.at[j], wu.at[slot], wsem.at[1, slot]))

    def w_d(j, slot):
        return pltpu.make_async_copy(wd_hbm.at[j], wd.at[slot], dsem.at[slot])

    def start_down():
        for j in range(ND):
            w_d(j, j).start()

    for j in range(NB):
        for copy in w_gu(j, j):
            copy.start()
    if not LINE:
        start_down()

    barrier = pltpu.get_barrier_semaphore()

    @pl.when(has_left)
    def _():
        pl.semaphore_signal(barrier, inc=1, device_id={"expert": e - 1}, device_id_type=MESH)

    @pl.when(has_right)
    def _():
        pl.semaphore_signal(barrier, inc=1, device_id={"expert": e + 1}, device_id_type=MESH)

    pl.semaphore_signal(barrier, inc=1, device_id={"dp": mate}, device_id_type=MESH)
    for k in range(1, M):
        pl.semaphore_signal(
            barrier, inc=1, device_id={"dp": 2 * across(k) + c}, device_id_type=MESH)

    route[e, :top] = ids_ref[...].astype(F32)
    route[e, top:] = sco_ref[...]
    xall[e] = tok_ref[...]

    def routing(block, pair, side):
        affinity = 1.0 / (1.0 + jnp.exp(-route[block, top:]))
        weights = 2.5 * affinity / jnp.sum(affinity, axis=0, keepdims=True)
        number = lax.broadcasted_iota(jnp.int32, (EP, tok), 0) + e * EL
        number = number.astype(F32)
        routed = jnp.zeros((EP, tok), F32)
        weight = jnp.zeros((EP, tok), F32)
        for k in range(top):
            hit = route[block, k:k + 1] == number
            routed = routed + jnp.where(hit, 1.0, 0.0)
            weight = weight + jnp.where(hit, weights[k:k + 1, :], 0.0)
        earlier = (lax.broadcasted_iota(jnp.int32, (tok, tok), 0)
                   < lax.broadcasted_iota(jnp.int32, (tok, tok), 1))
        rank = dot(routed.astype(BF16), jnp.where(earlier, 1.0, 0.0).astype(BF16))
        first = jnp.asarray((2 * pair + side) * CAP, F32)
        lanes = slice(side * tok, (side + 1) * tok)
        slot_c[pair, :, lanes] = jnp.where(routed > 0.5, rank + first, -1.0)
        wgt_c[pair, :, lanes] = weight

    acc[...] = jnp.zeros_like(acc)
    if LINE:
        routing(e, 0, 0)

    with jax.named_scope("barrierw"):
        pl.semaphore_wait(barrier, M + has_left.astype(jnp.int32) + has_right.astype(jnp.int32))

    def gather_to(s, side, target, parts=(0, 1, 2)):
        copies = []
        for p in parts:
            ref = route.at[s] if p == 0 else xall.at[s, pl.ds((p - 1) * half, half)]
            copies.append(remote(ref, ref, ag_s.at[side, p, s], ag_r.at[p, s], expert=target))
        return copies

    def start_right(s, parts=(0, 1, 2)):
        @pl.when(has_right)
        def _():
            for copy in gather_to(s, 0, e + 1, parts):
                copy.start()

    def start_left(s, parts=(0, 1, 2)):
        @pl.when(has_left)
        def _():
            for copy in gather_to(s, 1, e - 1, parts):
                copy.start()

    def gather_step(k, parts=(0, 1, 2)):
        @pl.when(e - k >= 0)
        def _():
            for copy in gather_to(e - k, 0, e, parts):
                copy.wait_recv()
            start_right(e - k, parts)

        @pl.when(e + k <= E - 1)
        def _():
            for copy in gather_to(e + k, 1, e, parts):
                copy.wait_recv()
            start_left(e + k, parts)

    def arrived(s, parts=(0, 1, 2)):
        for copy in gather_to(s, 0, e, parts):
            copy.wait_recv()

    for parts in ((0, 1), (2,)):
        start_right(e, parts)
        start_left(e, parts)

    if LINE:
        with jax.named_scope("gather1"):
            for parts in ((0, 1), (2,)):
                gather_step(1, parts)
            routing(nb, 0, 1)
    else:
        def whole_step(k, carry):
            gather_step(k)
            return carry

        def list_pair(p, carry):
            routing(2 * p, p, 0)
            routing(2 * p + 1, p, 1)
            return carry

        lax.fori_loop(1, E, whole_step, 0)
        lax.fori_loop(0, E // 2, list_pair, 0)

    class Item:
        def __init__(self, j, q, parts):
            self.j, self.q, self.parts = j, q, parts
            self.group = G // parts
            self.rows, self.toks = R // parts, T // parts
            self.buf = j if NCH == 1 else j * NCH + q
            if parts == 1:
                self.sem = 2 * self.buf
                self.span = pl.ds(0, R)
                self.first = 0 if LINE else q * R
            else:
                self.sem = 2 * j + q
                self.span = pl.ds(pl.multiple_of(q * self.rows, self.rows), self.rows)
                self.first = q * self.rows
            if not LINE:
                self.blocks = [q * G + i for i in range(G)]
            elif parts == 1:
                self.blocks = order
            else:
                self.blocks = [jnp.where(q == 0, e, fa), jnp.where(q == 0, nb, fb)]

        def pieces(self):
            if LINE and self.parts == 1:
                return [Item(self.j, 1, 2), Item(self.j, 0, 2)]
            return [self]

        def row(self, table):
            pairs = self.group // 2
            at = 0 if LINE and self.parts == 1 else self.q * pairs
            return jnp.concatenate(
                [table[at + p, pl.ds(self.j, 1), :] for p in range(pairs)], axis=1)

    def taken(it):
        row = it.row(slot_c)
        return (row.astype(jnp.int32) - it.first
                == lax.broadcasted_iota(jnp.int32, (it.rows, it.toks), 0))

    def pair_copy(it):
        return remote(s1.at[it.buf, :, it.span], r1.at[it.buf, :, it.span],
                      p_s, p_r.at[it.sem], dp=mate)

    def sum_copy(it, k):
        return remote(s2.at[it.buf, k - 1, it.span], r2.at[it.buf, k - 1, it.span],
                      q_s, q_r.at[it.sem, k], dp=2 * across(k) + c)

    def share_copy(it, k):
        return remote(hid.at[it.buf, d, it.span], hid.at[it.buf, d, it.span],
                      h_s, h_r.at[it.sem, k], dp=2 * across(k) + c)

    def mate_copy(it, k):
        block = 2 * source(k) + c
        return remote(hid.at[it.buf, block, it.span], hid.at[it.buf, block, it.span],
                      h_s, f_r.at[it.sem, k], dp=mate)

    def stage_a(it, first, last):
        j, span = it.j, it.span
        slot = lax.rem(j, NB)

        @pl.when(first)
        def _():
            for copy in w_gu(j, slot):
                copy.wait()

        pick = jnp.where(taken(it), 1.0, 0.0).astype(BF16)
        for at in range(0, width, ct):
            xq = jnp.concatenate([xall[b, :, at:at + ct] for b in it.blocks], axis=0)
            rows[:it.rows, at:at + ct] = dot(pick, xq).astype(BF16)

        def block(m, core):
            cols = pl.ds(pl.multiple_of((2 * m + core) * hb, hb), hb)
            xr = rows[:it.rows, :]
            return dot(xr, wg[slot, :, cols]), dot(xr, wu[slot, :, cols])

        for m in range(M):
            g, u = block(m, 1 - c)
            s1[it.buf, m, span, :hb] = g.astype(BF16)
            s1[it.buf, m, span, hb:] = u.astype(BF16)
        for piece in it.pieces():
            pair_copy(piece).start()
        for m in range(M):
            g, u = block(m, c)
            keep[it.buf, m, span, :hb] = g.astype(BF16)
            keep[it.buf, m, span, hb:] = u.astype(BF16)

        @pl.when(last & (j + NB < EL))
        def _():
            for copy in w_gu(j + NB, slot):
                copy.start()

    def stage_b(it):
        i, span = it.buf, it.span
        pair_copy(it).wait_recv()
        for k in range(1, M):
            to = across(k)
            s2[i, k - 1, span] = (keep[i, to, span].astype(F32)
                                  + r1[i, to, span].astype(F32)).astype(BF16)
            sum_copy(it, k).start()

    def stage_c(it):
        i, span = it.buf, it.span
        total = keep[i, x, span].astype(F32) + r1[i, x, span].astype(F32)
        for k in range(1, M):
            sum_copy(it, k).wait_recv()
            total = total + r2[i, k - 1, span].astype(F32)
        g, u = total[:, :hb], total[:, hb:]
        hid[i, d, span] = (g / (1.0 + jnp.exp(-g)) * u).astype(BF16)
        for k in range(1, M):
            share_copy(it, k).start()
        mate_copy(it, 0).start()

    def stage_d(it):
        for k in range(1, M):
            share_copy(it, k).wait_recv()
            mate_copy(it, k).start()

    def stage_e(it, first, last):
        j, span = it.j, it.span
        slot = lax.rem(j, ND)

        @pl.when(first)
        def _():
            w_d(j, slot).wait()

        for piece in it.pieces():
            for k in range(M):
                mate_copy(piece, k).wait_recv()
        hit = taken(it)
        scale = jnp.sum(jnp.where(hit, it.row(wgt_c), 0.0), axis=1, keepdims=True)
        pick = jnp.where(hit, 1.0, 0.0).astype(BF16)
        hidden = jnp.concatenate([hid[it.buf, b, span] for b in range(DP)], axis=1)
        for at in range(0, width, ct):
            out = (dot(hidden, wd[slot, :, at:at + ct]) * scale).astype(BF16)
            add = dot(pick, out, ((0,), (0,)))
            for i, b in enumerate(it.blocks):
                acc[b, :, at:at + ct] += add[i * tok:(i + 1) * tok]

        @pl.when(last & (j + ND < EL))
        def _():
            w_d(j + ND, slot).start()

    def tail(way, s, n, target):
        part = pl.ds(n * half, half)
        return remote(rs_s.at[s, part], rs_in.at[way, s, part],
                      t_s.at[s, n], t_r.at[way, s, n], expert=target)

    def pass_on(way, s, n, target, adds):
        part = pl.ds(n * half, half)
        if adds is None:
            rs_s[s, part] = acc[s, part].astype(BF16)
        else:
            @pl.when(adds)
            def _():
                tail(way, s, n, e).wait_recv()
                rs_s[s, part] = (acc[s, part] + rs_in[way, s, part].astype(F32)).astype(BF16)

            @pl.when(jnp.logical_not(adds))
            def _():
                rs_s[s, part] = acc[s, part].astype(BF16)
        tail(way, s, n, target).start()

    if LINE:
        B, C, D, L = LINE_LAGS[1:]

        def piece(t):
            far = (t >= K) & (t < 3 * K)
            j = t - jnp.where(t >= K, K, 0) - jnp.where(t >= 3 * K, K, 0)
            return Item(j, jnp.where(far, 1, 0), 2)

        def step(i, carry):
            @pl.when(i == K)
            def _():
                with jax.named_scope("gather3"):
                    @pl.when(jnp.logical_not(mid))
                    def _():
                        arrived(fa)
                        arrived(fb)

                    routing(fa, 1, 0)
                    routing(fb, 1, 1)

            @pl.when(i < 2 * K)
            def _():
                with jax.named_scope("stage_a"):
                    it = piece(i)
                    stage_a(it, i < K, i >= K)

            @pl.when((i >= 2 * K) & (i < 3 * K))
            def _():
                with jax.named_scope("stage_a"):
                    stage_a(Item(i - K, 0, 1), i >= 0, i >= 0)

            @pl.when(i == 0)
            def _():
                start_down()

            for n, parts in enumerate(((0, 1), (2,))):
                @pl.when((i == n) & mid)
                def _(parts=parts):
                    with jax.named_scope("gather2"):
                        arrived(fb, parts)
                        for copy in gather_to(fb, 1 - onward, 3 - fb, parts):
                            copy.start()

            for lag, stage in ((B, stage_b), (C, stage_c), (D, stage_d)):
                @pl.when((i >= lag) & (i < 4 * K + lag))
                def _(lag=lag, stage=stage):
                    with jax.named_scope(stage.__name__):
                        stage(piece(i - lag))

            t = i - L

            @pl.when((t >= K) & (t < 2 * K))
            def _():
                with jax.named_scope("stage_e"):
                    stage_e(Item(t - K, 0, 1), t >= 0, t >= 0)

            @pl.when(t >= 2 * K)
            def _():
                with jax.named_scope("stage_e"):
                    it = piece(t)
                    stage_e(it, t < 3 * K, t < 0)

            @pl.when((t == 3 * K - 1) & jnp.logical_not(mid))
            def _():
                with jax.named_scope("r0"):
                    for s in (fb, fa):
                        for n in range(2):
                            pass_on(onward, s, n, nb, None)

            for n in range(2):
                @pl.when((t == 4 * K - 3 + n) & mid)
                def _(n=n):
                    with jax.named_scope("r1"):
                        pass_on(onward, fb, n, nb, t >= 0)
            return carry

        lax.fori_loop(0, 4 * K + L, step, 0)

        with jax.named_scope("r2"):
            for n in range(2):
                pass_on(onward, nb, n, nb, mid)

            @pl.when(mid)
            def _():
                for n in range(2):
                    pass_on(1 - onward, fa, n, fa, e >= 0)
    else:
        stages = (lambda it: stage_a(it, first_of(it), last_of(it)), stage_b, stage_c, stage_d,
                  lambda it: stage_e(it, first_of(it), last_of(it)))

        def first_of(it):
            return it.q == 0

        def last_of(it):
            return it.q == NCH - 1

        def item(t):
            return Item(lax.div(t, NCH), lax.rem(t, NCH), 1)

        def step(i, carry):
            for stage, lag in zip(stages, LAGS):
                @pl.when((i >= lag) & (i < N + lag))
                def _(stage=stage, lag=lag):
                    stage(item(i - lag))
            return carry

        lax.fori_loop(0, N + LAGS[-1], step, 0)

        def tail_step(t, carry):
            far, near = E - 1 - t, t
            for n in range(2):
                @pl.when((far > e) & has_right)
                def _(n=n):
                    pass_on(0, far, n, e + 1, has_left)

                @pl.when((near < e) & has_left)
                def _(n=n):
                    pass_on(1, near, n, e - 1, has_right)
            return carry

        lax.fori_loop(0, E - 1, tail_step, 0)

    with jax.named_scope("drain"):
        def drain_line(s, carry):
            for p in range(3):
                @pl.when((s <= e) & has_right)
                def _(p=p):
                    gather_to(s, 0, e, (p,))[0].wait_send()

                @pl.when((s >= e) & has_left)
                def _(p=p):
                    gather_to(s, 1, e, (p,))[0].wait_send()
            return carry

        lax.fori_loop(0, E, drain_line, 0)
        remote(s1, r1, p_s, p_r.at[0], dp=mate).wait_send()
        remote(s2, r2, q_s, q_r.at[0, 1], dp=mate).wait_send()
        sent = hid.at[:, pl.ds(0, 2 * M - 1)]
        remote(sent, sent, h_s, h_r.at[0, 1], dp=mate).wait_send()

    with jax.named_scope("own"):
        for n in range(2):
            part = pl.ds(n * half, half)
            for way, has in ((0, has_left), (1, has_right)):
                @pl.when(has)
                def _(way=way):
                    tail(way, e, n, e).wait_recv()
                    acc[e, part] = acc[e, part] + rs_in[way, e, part].astype(F32)

            out_ref[part] = acc[e, part].astype(BF16)

        def drain_sums(s, carry):
            @pl.when(s != e)
            def _():
                for n in range(2):
                    tail(0, s, n, e).wait_send()
            return carry

        lax.fori_loop(0, E, drain_sums, 0)


def on_device(tokens, expert_ids, scores, w_gate, w_up, w_down):
    E, DP = lax.axis_size("expert"), lax.axis_size("dp")
    tok, width = tokens.shape
    top = expert_ids.shape[1]
    EL, _, H = w_gate.shape
    n_exp = E * EL
    CAP = 2 * tok * top // n_exp
    G = min(E, 4)
    NCH = E // G
    LINE = E == 4 and EL % 2 == 0 and EL >= 4
    NB = EL // 2 if LINE else min(3, EL)
    ND = EL // 2 + 2 if LINE else min(3, EL)
    ct = tile_of(width)
    M, hb, R, N = DP // 2, H // DP, G * CAP, EL * NCH
    EP = max(EL, 8)
    vmem, dma = pltpu.VMEM, pltpu.SemaphoreType.DMA
    scratch = [
        vmem((NB, width, H), BF16), vmem((NB, width, H), BF16), vmem((ND, H, width), BF16),
        vmem((E, tok, width), BF16), vmem((E, 2 * top, tok), F32),
        vmem((E // 2, EP, 2 * tok), F32), vmem((E // 2, EP, 2 * tok), F32),
        vmem((R, width), BF16),
        vmem((N, M, R, 2 * hb), BF16), vmem((N, M, R, 2 * hb), BF16),
        vmem((N, M, R, 2 * hb), BF16),
        vmem((N, M - 1, R, 2 * hb), BF16), vmem((N, M - 1, R, 2 * hb), BF16),
        vmem((N, DP, R, hb), BF16),
        vmem((E, tok, width), F32),
        vmem((E, tok, width), BF16), vmem((2, E, tok, width), BF16),
        dma((2, NB)), dma((ND,)), dma((2, 3, E)), dma((3, E)),
        dma(()), dma((2 * N,)), dma(()), dma((2 * N, M)), dma(()), dma((2 * N, M)),
        dma((2 * N, M)),
        dma((E, 2)), dma((2, E, 2)),
    ]
    whole = pl.BlockSpec(memory_space=pltpu.VMEM)
    hbm = pl.BlockSpec(memory_space=pl.ANY)
    return pl.pallas_call(
        functools.partial(kernel, (E, DP, EL, NCH, G, CAP, NB, ND, LINE, ct)),
        out_shape=jax.ShapeDtypeStruct((tok, width), BF16),
        in_specs=[whole] * 3 + [hbm] * 3,
        out_specs=whole,
        scratch_shapes=scratch,
        compiler_params=pltpu.CompilerParams(
            collective_id=0, has_side_effects=True, vmem_limit_bytes=62 * 2**20),
        name="routed_experts",
    )(tokens, expert_ids.T, scores.T, w_gate, w_up, w_down)


def solution(mesh):
    in_specs = (
        P(("groups", "expert"), "dp"),
        P(("groups", "expert"), None),
        P(("groups", "expert"), None),
        P("expert", "dp", None),
        P("expert", "dp", None),
        P("expert", None, "dp"),
    )
    out_specs = P(("groups", "expert"), "dp")
    return jax.shard_map(
        on_device, mesh=mesh, in_specs=in_specs, out_specs=out_specs, check_vma=False
    )
```

```python
import functools

import jax
import jax.numpy as jnp
from jax import lax
from jax.experimental import pallas as pl
from jax.experimental.pallas import tpu as pltpu
from jax.sharding import PartitionSpec as P

MESH = pl.DeviceIdType.MESH
F32, BF16 = jnp.float32, jnp.bfloat16
LAGS = (0, 1, 3, 5, 7)
A, B, C, D, E, X = (32 * stage for stage in range(1, 7))
ORDER = (
    A, X, A + 1, X + 1, B, B + 1, A + 2, B + 2, A + 3, B + 3, C, C + 1, C + 2, X + 2, A + 4,
    C + 3, A + 5, B + 4, A + 6, B + 5, B + 6, A + 7, D, B + 7, D + 1, C + 4, A + 8, C + 5,
    D + 2, B + 8, C + 6, A + 9, C + 7, A + 10, B + 9, D + 3, D + 4, B + 10, A + 11, C + 8,
    D + 5, E, D + 6, B + 11, E + 1, D + 7, C + 9, C + 10, B + 12, E + 2, D + 8, E + 3, C + 11,
    D + 9, B + 13, E + 4, D + 10, B + 14, B + 15, E + 5, C + 12, D + 11, E + 6, E + 7, X + 3,
    C + 13, C + 14, C + 15, D + 12, D + 13, E + 8, X + 4, D + 14, D + 15, E + 9, E + 10, X + 5,
    E + 11,
)


def packed(codes):
    codes = codes + (0,) * (-len(codes) % 3)
    return [sum(code * 256 ** i for i, code in enumerate(codes[at:at + 3]))
            for at in range(0, len(codes), 3)]


def dot(a, b, dims=((1,), (0,))):
    return lax.dot_general(a, b, (dims, ((), ())), preferred_element_type=F32)


def remote(src, dst, send, recv, **where):
    return pltpu.make_async_remote_copy(
        src_ref=src, dst_ref=dst, send_sem=send, recv_sem=recv,
        device_id=where, device_id_type=MESH,
    )


def tile_of(size):
    for tile in (512, 384, 256, 128):
        if size % tile == 0:
            return tile
    return size


def kernel(dims, tok_hbm, ids_ref, sco_ref, wg_hbm, wu_hbm, wd_hbm, out_hbm,
           wg, wu, wd, xall, route, slot_c, wgt_c, rows, s1, r1, keep, s2, r2, hid, acc,
           rs_s, rs_in, out_v,
           io_sem, wsem, dsem, ag_s, ag_r, p_s, p_r, q_s, q_r, h_s, h_r, f_r, t_s, t_r):
    E, DP, EL, NCH, G, CAP, NB, ND, LINE, ct = dims
    M = DP // 2
    tok, width = tok_hbm.shape
    top = ids_ref.shape[0]
    H = wg.shape[2]
    hb = H // DP
    R, T = G * CAP, G * tok
    N = EL * NCH
    K = EL // 2
    half = tok // 2
    EP = slot_c.shape[1]
    e = lax.axis_index("expert")
    d = lax.axis_index("dp")
    x, c = lax.div(d, 2), lax.rem(d, 2)
    mate = 2 * x + 1 - c
    has_left, has_right = e > 0, e < E - 1
    if LINE:
        low = e < 2
        mid = (e == 1) | (e == 2)
        onward = jnp.where(low, 0, 1)
        nb = jnp.where(low, e + 1, e - 1)
        fb = jnp.where(low, 3, 0)
        fa = 6 - e - nb - fb
        order = (e, nb, fa, fb)

    def across(k):
        return lax.rem(x + k, M)

    def source(k):
        return lax.rem(x + M - k, M)

    def w_gu(j, slot):
        return (pltpu.make_async_copy(wg_hbm.at[j], wg.at[slot], wsem.at[0, slot]),
                pltpu.make_async_copy(wu_hbm.at[j], wu.at[slot], wsem.at[1, slot]))

    def w_d(j, slot):
        return pltpu.make_async_copy(wd_hbm.at[j], wd.at[slot], dsem.at[slot])

    def start_down():
        for j in range(ND):
            w_d(j, j).start()

    own_rows = pltpu.make_async_copy(tok_hbm, xall.at[e], io_sem.at[0])
    own_rows.start()
    def start_up(*experts):
        for j in experts:
            for copy in w_gu(j, j):
                copy.start()

    if not LINE:
        start_up(*range(NB))
        start_down()

    barrier = pltpu.get_barrier_semaphore()

    @pl.when(has_left)
    def _():
        pl.semaphore_signal(barrier, inc=1, device_id={"expert": e - 1}, device_id_type=MESH)

    @pl.when(has_right)
    def _():
        pl.semaphore_signal(barrier, inc=1, device_id={"expert": e + 1}, device_id_type=MESH)

    pl.semaphore_signal(barrier, inc=1, device_id={"dp": mate}, device_id_type=MESH)
    for k in range(1, M):
        pl.semaphore_signal(
            barrier, inc=1, device_id={"dp": 2 * across(k) + c}, device_id_type=MESH)

    route[e, :top] = ids_ref[...].astype(F32)
    route[e, top:] = sco_ref[...]

    def routing(block, pair, side):
        affinity = 1.0 / (1.0 + jnp.exp(-route[block, top:]))
        weights = 2.5 * affinity / jnp.sum(affinity, axis=0, keepdims=True)
        number = lax.broadcasted_iota(jnp.int32, (EP, tok), 0) + e * EL
        number = number.astype(F32)
        routed = jnp.zeros((EP, tok), F32)
        weight = jnp.zeros((EP, tok), F32)
        for k in range(top):
            hit = route[block, k:k + 1] == number
            routed = routed + jnp.where(hit, 1.0, 0.0)
            weight = weight + jnp.where(hit, weights[k:k + 1, :], 0.0)
        earlier = (lax.broadcasted_iota(jnp.int32, (tok, tok), 0)
                   < lax.broadcasted_iota(jnp.int32, (tok, tok), 1))
        rank = dot(routed.astype(BF16), jnp.where(earlier, 1.0, 0.0).astype(BF16))
        lanes = slice(side * tok, (side + 1) * tok)
        slot_c[pair, :, lanes] = jnp.where(routed > 0.5, rank + float(side * CAP), -float(R))
        wgt_c[pair, :, lanes] = weight

    acc[...] = jnp.zeros_like(acc)
    if LINE:
        routing(e, 0, 0)
    own_rows.wait()
    if LINE:
        start_up(0, 1)

    with jax.named_scope("barrierw"):
        pl.semaphore_wait(barrier, M + has_left.astype(jnp.int32) + has_right.astype(jnp.int32))

    def sent_sem(side, p, s):
        return ag_s.at[side, min(p, 1)] if LINE else ag_s.at[side, p, s]

    def gather_to(s, side, target, parts=(0, 1, 2)):
        copies = []
        for p in parts:
            ref = route.at[s] if p == 0 else xall.at[s, pl.ds((p - 1) * half, half)]
            copies.append(remote(ref, ref, sent_sem(side, p, s), ag_r.at[p, s], expert=target))
        return copies

    def start_right(s, parts=(0, 1, 2)):
        @pl.when(has_right)
        def _():
            for copy in gather_to(s, 0, e + 1, parts):
                copy.start()

    def start_left(s, parts=(0, 1, 2)):
        @pl.when(has_left)
        def _():
            for copy in gather_to(s, 1, e - 1, parts):
                copy.start()

    def gather_step(k, parts=(0, 1, 2)):
        @pl.when(e - k >= 0)
        def _():
            for copy in gather_to(e - k, 0, e, parts):
                copy.wait_recv()
            start_right(e - k, parts)

        @pl.when(e + k <= E - 1)
        def _():
            for copy in gather_to(e + k, 1, e, parts):
                copy.wait_recv()
            start_left(e + k, parts)

    def arrived(s, parts=(0, 1, 2)):
        for copy in gather_to(s, 0, e, parts):
            copy.wait_recv()

    for parts in ((0, 1), (2,)):
        start_right(e, parts)
        start_left(e, parts)

    if not LINE:
        def whole_step(k, carry):
            gather_step(k)
            return carry

        def list_pair(p, carry):
            routing(2 * p, p, 0)
            routing(2 * p + 1, p, 1)
            return carry

        lax.fori_loop(1, E, whole_step, 0)
        lax.fori_loop(0, E // 2, list_pair, 0)

    class Item:
        def __init__(self, j, pos, n, q=0):
            self.j, self.n, self.q = j, n, q
            self.rows, self.toks = n * CAP, n * tok
            self.buf = j * NCH + q
            self.sem = 2 * self.buf + (pos // 2 if isinstance(pos, int) else lax.div(pos, 2))
            start = pos * CAP if isinstance(pos, int) else pl.multiple_of(pos * CAP, n * CAP)
            self.span = pl.ds(start, self.rows)
            first = q * (G // 2) + (pos // 2 if isinstance(pos, int) else lax.div(pos, 2))
            self.pairs = [first + i for i in range(n // 2)]
            if not LINE:
                self.blocks = [q * G + i for i in range(n)]
            elif n == 4:
                self.blocks = order
            else:
                self.blocks = [jnp.where(pos == 0, e, fa), jnp.where(pos == 0, nb, fb)]

        def pieces(self):
            if not LINE or self.n < 4:
                return [self]
            return [Item(self.j, p, n) for p, n in self.cut]

        def row(self, table, step):
            return jnp.concatenate(
                [table[p, pl.ds(self.j, 1), :] + 2 * step * i
                 for i, p in enumerate(self.pairs)], axis=1)

    def taken(it):
        row = it.row(slot_c, float(CAP))
        return (row.astype(jnp.int32)
                == lax.broadcasted_iota(jnp.int32, (it.rows, it.toks), 0))

    def pair_copy(it):
        return remote(s1.at[it.buf, :, it.span], r1.at[it.buf, :, it.span],
                      p_s, p_r.at[it.sem], dp=mate)

    def sum_copy(it, k):
        return remote(s2.at[it.buf, k - 1, it.span], r2.at[it.buf, k - 1, it.span],
                      q_s, q_r.at[it.sem, k - 1], dp=2 * across(k) + c)

    def share_copy(it, k):
        return remote(hid.at[it.buf, d, it.span], hid.at[it.buf, d, it.span],
                      h_s, h_r.at[it.sem, k - 1], dp=2 * across(k) + c)

    def mate_copy(it, k):
        block = 2 * source(k) + c
        return remote(hid.at[it.buf, block, it.span], hid.at[it.buf, block, it.span],
                      h_s, f_r.at[it.sem], dp=mate)

    def stage_a(it, first, last):
        j, span = it.j, it.span
        slot = lax.rem(j, NB)

        pick = jnp.where(taken(it), 1.0, 0.0).astype(BF16)

        @pl.when(first)
        def _():
            for copy in w_gu(j, slot):
                copy.wait()

        for at in range(0, width, ct):
            xq = jnp.concatenate([xall[b, :, at:at + ct] for b in it.blocks], axis=0)
            rows[:it.rows, at:at + ct] = dot(pick, xq).astype(BF16)

        def block(m, core):
            cols = pl.ds(pl.multiple_of((2 * m + core) * hb, hb), hb)
            xr = rows[:it.rows, :]
            return dot(xr, wg[slot, :, cols]), dot(xr, wu[slot, :, cols])

        for m in range(M):
            g, u = block(m, 1 - c)
            s1[it.buf, m, span, :hb] = g.astype(BF16)
            s1[it.buf, m, span, hb:] = u.astype(BF16)
        for piece in it.pieces():
            pair_copy(piece).start()
        for m in range(M):
            g, u = block(m, c)
            keep[it.buf, m, span, :hb] = g.astype(BF16)
            keep[it.buf, m, span, hb:] = u.astype(BF16)

        @pl.when(last & (j + NB < EL))
        def _():
            for copy in w_gu(j + NB, slot):
                copy.start()

    def stage_b(it):
        i, span = it.buf, it.span
        pair_copy(it).wait_recv()
        for k in range(1, M):
            to = across(k)
            s2[i, k - 1, span] = (keep[i, to, span].astype(F32)
                                  + r1[i, to, span].astype(F32)).astype(BF16)
            sum_copy(it, k).start()

    def stage_c(it):
        i, span = it.buf, it.span
        total = keep[i, x, span].astype(F32) + r1[i, x, span].astype(F32)
        for k in range(1, M):
            sum_copy(it, k).wait_recv()
            total = total + r2[i, k - 1, span].astype(F32)
        g, u = total[:, :hb], total[:, hb:]
        hid[i, d, span] = (g / (1.0 + jnp.exp(-g)) * u).astype(BF16)
        for k in range(1, M):
            share_copy(it, k).start()
        mate_copy(it, 0).start()

    def stage_d(it):
        for k in range(1, M):
            share_copy(it, k).wait_recv()
            mate_copy(it, k).start()

    def stage_e(it, first, last):
        j, span = it.j, it.span
        slot = lax.rem(j, ND)
        hit = taken(it)
        scale = jnp.sum(jnp.where(hit, it.row(wgt_c, 0.0), 0.0), axis=1, keepdims=True)
        pick = jnp.where(hit, 1.0, 0.0).astype(BF16)

        @pl.when(first)
        def _():
            w_d(j, slot).wait()

        for piece in it.pieces():
            both = hid.at[it.buf, pl.ds(0, M), piece.span]
            remote(both, both, h_s, f_r.at[piece.sem], dp=mate).wait_recv()
        hidden = jnp.concatenate([hid[it.buf, b, span] for b in range(DP)], axis=1)

        def add_to(at, out):
            add = dot(pick, out, ((0,), (0,)))
            for i, b in enumerate(it.blocks):
                acc[b, :, at:at + ct] += add[i * tok:(i + 1) * tok]

        held = None
        for at in range(0, width, ct):
            out = (dot(hidden, wd[slot, :, at:at + ct]) * scale).astype(BF16)
            if held is not None:
                add_to(*held)
            held = (at, out)
        add_to(*held)

        @pl.when(last & (j + ND < EL))
        def _():
            w_d(j + ND, slot).start()

    def tail(at, s, n, target):
        part = pl.ds(n * half, half)
        return remote(rs_s.at[s, part], rs_in.at[at, part],
                      t_s if LINE else t_s.at[s, n], t_r.at[at, n], expert=target)

    def pass_on(to, s, n, target, have, adds):
        part = pl.ds(n * half, half)

        def alone():
            rs_s[s, part] = acc[s, part].astype(BF16)

        if adds is None:
            alone()
        else:
            pl.when(jnp.logical_not(adds))(alone)

            @pl.when(adds)
            def _():
                tail(have, s, n, e).wait_recv()
                rs_s[s, part] = (acc[s, part] + rs_in[have, part].astype(F32)).astype(BF16)

        tail(to, s, n, target).start()

    if LINE:
        with jax.named_scope("gather1"):
            gather_step(1, (0, 1))
            start_up(*range(2, NB))
            gather_step(1, (2,))
            routing(nb, 0, 1)

        def half_item(t):
            far = (t >= K) & (t < 3 * K)
            j = t - jnp.where(t >= K, K, 0) - jnp.where(t >= 3 * K, K, 0)
            return Item(j, jnp.where(far, 2, 0), 2)

        def full_item(j):
            it = Item(j, 0, 4)
            it.cut = ((2, 2), (0, 2))
            return it

        def run_a(u):
            @pl.when(u < 2 * K)
            def _():
                stage_a(half_item(u), u < K, u >= K)

            @pl.when(u >= 2 * K)
            def _():
                stage_a(full_item(u - K), u >= 0, u >= 0)

        def run_e(u):
            @pl.when(u < K)
            def _():
                stage_e(full_item(u), u >= 0, u >= 0)

            @pl.when(u >= K)
            def _():
                stage_e(half_item(u + K), u < 2 * K, u < 0)

        def event(u):
            for n, parts in enumerate(((0, 1), (2,))):
                @pl.when((u == n) & mid)
                def _(parts=parts):
                    arrived(fb, parts)
                    for copy in gather_to(fb, 1 - onward, 3 - fb, parts):
                        copy.start()

                @pl.when((u == 4 + n) & mid)
                def _(n=n):
                    pass_on(1, fb, n, fb, 0, u >= 0)

            @pl.when(u == 0)
            def _():
                start_down()

            @pl.when(u == 2)
            def _():
                @pl.when(jnp.logical_not(mid))
                def _():
                    arrived(fa)
                    arrived(fb)

                routing(fa, 1, 0)
                routing(fb, 1, 1)

            @pl.when((u == 3) & jnp.logical_not(mid))
            def _():
                for s, to in ((fb, 0), (fa, 2)):
                    for n in range(2):
                        pass_on(to, s, n, nb, None, None)

            @pl.when((u == 3) & mid)
            def _():
                for n in range(2):
                    pass_on(0, fa, n, fa, None, None)

        runs = (run_a, lambda t: stage_b(half_item(t)), lambda t: stage_c(half_item(t)),
                lambda t: stage_d(half_item(t)), run_e, event)
        words = packed(ORDER)

        def four(w, carry):
            word = jnp.int32(words[0])
            for i, value in enumerate(words[1:]):
                word = jnp.where(w == i + 1, value, word)

            def one(i, word):
                code = lax.rem(word, 256)
                stage, arg = lax.div(code, 32), lax.rem(code, 32)
                for i, run in enumerate(runs):
                    @pl.when(stage == i + 1)
                    def _(i=i, run=run):
                        with jax.named_scope("ABCDEX"[i]):
                            run(arg)
                return lax.div(word, 256)

            lax.fori_loop(0, 3, one, word)
            return carry

        lax.fori_loop(0, len(words), four, 0)

        with jax.named_scope("r2"):
            for n in range(2):
                pass_on(jnp.where(mid, 4, 3), nb, n, nb, 2, mid)
    else:
        stages = (lambda it: stage_a(it, first_of(it), last_of(it)), stage_b, stage_c, stage_d,
                  lambda it: stage_e(it, first_of(it), last_of(it)))

        def first_of(it):
            return it.q == 0

        def last_of(it):
            return it.q == NCH - 1

        def item(t):
            return Item(lax.div(t, NCH), 0, G, lax.rem(t, NCH))

        def step(i, carry):
            for stage, lag in zip(stages, LAGS):
                @pl.when((i >= lag) & (i < N + lag))
                def _(stage=stage, lag=lag):
                    stage(item(i - lag))
            return carry

        lax.fori_loop(0, N + LAGS[-1], step, 0)

        def tail_step(t, carry):
            far, near = E - 1 - t, t
            for n in range(2):
                @pl.when((far > e) & has_right)
                def _(n=n):
                    pass_on(far, far, n, e + 1, far, has_left)

                @pl.when((near < e) & has_left)
                def _(n=n):
                    pass_on(E + near, near, n, e - 1, E + near, has_right)
            return carry

        lax.fori_loop(0, E - 1, tail_step, 0)

    with jax.named_scope("drain"):
        if LINE:
            for side, has, count in ((0, has_right, e + 1), (1, has_left, E - e)):
                for n in range(1, E):
                    @pl.when(has & (count == n))
                    def _(side=side, n=n):
                        for p, ref in enumerate((route, xall)):
                            ref = ref.at[pl.ds(0, n)]
                            remote(ref, ref, ag_s.at[side, p], ag_r.at[p, 0], expert=e).wait_send()
        else:
            def drain_line(s, carry):
                for p in range(3):
                    @pl.when((s <= e) & has_right)
                    def _(p=p):
                        gather_to(s, 0, e, (p,))[0].wait_send()

                    @pl.when((s >= e) & has_left)
                    def _(p=p):
                        gather_to(s, 1, e, (p,))[0].wait_send()
                return carry

            lax.fori_loop(0, E, drain_line, 0)
        remote(s1, r1, p_s, p_r.at[0], dp=mate).wait_send()
        remote(s2, r2, q_s, q_r.at[0, 0], dp=mate).wait_send()
        sent = hid.at[:, pl.ds(0, 2 * M - 1)]
        remote(sent, sent, h_s, h_r.at[0, 0], dp=mate).wait_send()

    def result(n):
        part = pl.ds(n * half, half)
        return pltpu.make_async_copy(out_v.at[part], out_hbm.at[part], io_sem.at[n])

    with jax.named_scope("own"):
        for n in range(2):
            part = pl.ds(n * half, half)
            if LINE:
                total = acc[e, part]
                for at in (jnp.where(mid, 3, 0), jnp.where(mid, 4, 1)):
                    tail(at, e, n, e).wait_recv()
                    total = total + rs_in[at, part].astype(F32)
                out_v[part] = total.astype(BF16)
            else:
                for at, has in ((e, has_left), (E + e, has_right)):
                    @pl.when(has)
                    def _(at=at):
                        tail(at, e, n, e).wait_recv()
                        acc[e, part] = acc[e, part] + rs_in[at, part].astype(F32)

                out_v[part] = acc[e, part].astype(BF16)
            result(n).start()

        if LINE:
            three = rs_s.at[pl.ds(0, E - 1)]
            remote(three, three, t_s, t_r.at[0, 0], expert=e).wait_send()
        else:
            def drain_sums(s, carry):
                @pl.when(s != e)
                def _():
                    for n in range(2):
                        tail(s, s, n, e).wait_send()
                return carry

            lax.fori_loop(0, E, drain_sums, 0)
        for n in range(2):
            result(n).wait()


def on_device(tokens, expert_ids, scores, w_gate, w_up, w_down):
    E, DP = lax.axis_size("expert"), lax.axis_size("dp")
    tok, width = tokens.shape
    top = expert_ids.shape[1]
    EL, _, H = w_gate.shape
    n_exp = E * EL
    CAP = 2 * tok * top // n_exp
    G = min(E, 4)
    NCH = E // G
    LINE = E == 4 and EL == 8
    NB = EL // 2 if LINE else min(3, EL)
    ND = EL // 2 + 2 if LINE else min(3, EL)
    ct = tile_of(width)
    M, hb, R, N = DP // 2, H // DP, G * CAP, EL * NCH
    EP = max(EL, 8)
    vmem, dma = pltpu.VMEM, pltpu.SemaphoreType.DMA
    scratch = [
        vmem((NB, width, H), BF16), vmem((NB, width, H), BF16), vmem((ND, H, width), BF16),
        vmem((E, tok, width), BF16), vmem((E, 2 * top, tok), F32),
        vmem((E // 2, EP, 2 * tok), F32), vmem((E // 2, EP, 2 * tok), F32),
        vmem((R, width), BF16),
        vmem((N, M, R, 2 * hb), BF16), vmem((N, M, R, 2 * hb), BF16),
        vmem((N, M, R, 2 * hb), BF16),
        vmem((N, M - 1, R, 2 * hb), BF16), vmem((N, M - 1, R, 2 * hb), BF16),
        vmem((N, DP, R, hb), BF16),
        vmem((E, tok, width), F32),
        vmem((E, tok, width), BF16), vmem((5 if LINE else 2 * E, tok, width), BF16),
        vmem((tok, width), BF16),
        dma((2,)), dma((2, NB)), dma((ND,)), dma((2, 2) if LINE else (2, 3, E)), dma((3, E)),
        dma(()), dma((2 * N,)), dma(()), dma((2 * N, M - 1)), dma(()), dma((2 * N, M - 1)),
        dma((2 * N,)),
        dma(() if LINE else (E, 2)), dma((5 if LINE else 2 * E, 2)),
    ]
    whole = pl.BlockSpec(memory_space=pltpu.VMEM)
    hbm = pl.BlockSpec(memory_space=pl.ANY)
    return pl.pallas_call(
        functools.partial(kernel, (E, DP, EL, NCH, G, CAP, NB, ND, LINE, ct)),
        out_shape=jax.ShapeDtypeStruct((tok, width), BF16),
        in_specs=[hbm] + [whole] * 2 + [hbm] * 3,
        out_specs=hbm,
        scratch_shapes=scratch,
        compiler_params=pltpu.CompilerParams(
            collective_id=0, has_side_effects=True, vmem_limit_bytes=62 * 2**20),
        name="routed_experts",
    )(tokens, expert_ids.T, scores.T, w_gate, w_up, w_down)


def solution(mesh):
    in_specs = (
        P(("groups", "expert"), "dp"),
        P(("groups", "expert"), None),
        P(("groups", "expert"), None),
        P("expert", "dp", None),
        P("expert", "dp", None),
        P("expert", None, "dp"),
    )
    out_specs = P(("groups", "expert"), "dp")
    return jax.shard_map(
        on_device, mesh=mesh, in_specs=in_specs, out_specs=out_specs, check_vma=False
    )
```

```python
import functools

import jax
import jax.numpy as jnp
from jax import lax
from jax.experimental import pallas as pl
from jax.experimental.pallas import tpu as pltpu
from jax.sharding import PartitionSpec as P

MESH = pl.DeviceIdType.MESH
F32, BF16 = jnp.float32, jnp.bfloat16
LAGS = (0, 1, 3, 5, 7)
A, E, X = 16, 32, 48
B, C, D = 16, 32, 48
ORDER = (
    (0, 0, 0, A), (0, 0, 0, X), (B, 0, 0, A + 1), (0, 0, 0, X + 1), (B + 1, 0, 0, A + 2),
    (C, B + 2, 0, A + 3), (C + 1, B + 3, 0, X + 2), (0, 0, 0, A + 4), (C + 2, D, B + 4, A + 5),
    (C + 3, D + 1, B + 5, A + 6), (C + 4, D + 2, B + 6, A + 7), (C + 5, D + 3, B + 7, A + 8),
    (C + 6, D + 4, B + 8, A + 9), (C + 7, D + 5, B + 9, A + 10), (C + 8, D + 6, B + 10, A + 11),
    (C + 9, D + 7, B + 11, 0), (B + 12, 0, 0, E), (C + 10, B + 13, 0, E + 1),
    (D + 8, 0, 0, E + 2), (C + 11, B + 14, D + 9, E + 3), (B + 15, 0, 0, E + 4),
    (D + 10, 0, 0, E + 5), (C + 12, D + 11, 0, E + 6), (C + 13, 0, 0, E + 7), (0, 0, 0, X + 3),
    (C + 14, D + 12, 0, E + 8), (C + 15, D + 13, 0, E + 9), (0, 0, 0, X + 4),
    (D + 14, 0, 0, E + 10), (D + 15, 0, 0, X + 5), (0, 0, 0, E + 11),
)


def packed(rows):
    return [a + 64 * (b + 64 * (c + 64 * d)) for a, b, c, d in rows]


def dot(a, b, dims=((1,), (0,))):
    return lax.dot_general(a, b, (dims, ((), ())), preferred_element_type=F32)


def remote(src, dst, send, recv, **where):
    return pltpu.make_async_remote_copy(
        src_ref=src, dst_ref=dst, send_sem=send, recv_sem=recv,
        device_id=where, device_id_type=MESH,
    )


def tile_of(size):
    for tile in (512, 384, 256, 128):
        if size % tile == 0:
            return tile
    return size


def kernel(dims, tok_hbm, ids_hbm, sco_hbm, wg_hbm, wu_hbm, wd_hbm, out_ref,
           wg, wu, wd, xall, route, slot_c, wgt_c, rows, s1, r1, keep, s2, r2, hid, acc,
           rs_s, rs_in, ids_ref, sco_ref,
           io_sem, wsem, dsem, ag_s, ag_r, p_s, p_r, q_s, q_r, h_s, h_r, f_r, t_s, t_r):
    E, DP, EL, NCH, G, CAP, NB, ND, LINE, ct = dims
    M = DP // 2
    tok, width = tok_hbm.shape
    top = ids_hbm.shape[0]
    H = wg.shape[2]
    hb = H // DP
    R, T = G * CAP, G * tok
    N = EL * NCH
    K = EL // 2
    half = tok // 2
    EP = slot_c.shape[1]
    e = lax.axis_index("expert")
    d = lax.axis_index("dp")
    x, c = lax.div(d, 2), lax.rem(d, 2)
    mate = 2 * x + 1 - c
    has_left, has_right = e > 0, e < E - 1
    if LINE:
        low = e < 2
        mid = (e == 1) | (e == 2)
        onward = jnp.where(low, 0, 1)
        nb = jnp.where(low, e + 1, e - 1)
        fb = jnp.where(low, 3, 0)
        fa = 6 - e - nb - fb
        order = (e, nb, fa, fb)

    def across(k):
        return lax.rem(x + k, M)

    def source(k):
        return lax.rem(x + M - k, M)

    def w_gu(j, slot):
        return (pltpu.make_async_copy(wg_hbm.at[j], wg.at[slot], wsem.at[0, slot]),
                pltpu.make_async_copy(wu_hbm.at[j], wu.at[slot], wsem.at[1, slot]))

    def w_d(j, slot):
        return pltpu.make_async_copy(wd_hbm.at[j], wd.at[slot], dsem.at[slot])

    def start_down():
        for j in range(ND):
            w_d(j, j).start()

    own_rows = pltpu.make_async_copy(tok_hbm, xall.at[e], io_sem.at[0])
    own_rows.start()
    own_ids = pltpu.make_async_copy(ids_hbm, ids_ref, io_sem.at[1])
    own_scores = pltpu.make_async_copy(sco_hbm, sco_ref, io_sem.at[2])
    own_ids.start()
    own_scores.start()
    def start_up(*experts):
        for j in experts:
            for copy in w_gu(j, j):
                copy.start()

    if not LINE:
        start_up(*range(NB))
        start_down()

    barrier = pltpu.get_barrier_semaphore()

    @pl.when(has_left)
    def _():
        pl.semaphore_signal(barrier, inc=1, device_id={"expert": e - 1}, device_id_type=MESH)

    @pl.when(has_right)
    def _():
        pl.semaphore_signal(barrier, inc=1, device_id={"expert": e + 1}, device_id_type=MESH)

    pl.semaphore_signal(barrier, inc=1, device_id={"dp": mate}, device_id_type=MESH)
    for k in range(1, M):
        pl.semaphore_signal(
            barrier, inc=1, device_id={"dp": 2 * across(k) + c}, device_id_type=MESH)

    acc[...] = jnp.zeros_like(acc)
    own_ids.wait()
    own_scores.wait()
    route[e, :top] = ids_ref[...].astype(F32)
    route[e, top:] = sco_ref[...]

    def routing(block, pair, side):
        affinity = 1.0 / (1.0 + jnp.exp(-route[block, top:]))
        weights = 2.5 * affinity / jnp.sum(affinity, axis=0, keepdims=True)
        number = lax.broadcasted_iota(jnp.int32, (EP, tok), 0) + e * EL
        number = number.astype(F32)
        routed = jnp.zeros((EP, tok), F32)
        weight = jnp.zeros((EP, tok), F32)
        for k in range(top):
            hit = route[block, k:k + 1] == number
            routed = routed + jnp.where(hit, 1.0, 0.0)
            weight = weight + jnp.where(hit, weights[k:k + 1, :], 0.0)
        earlier = (lax.broadcasted_iota(jnp.int32, (tok, tok), 0)
                   < lax.broadcasted_iota(jnp.int32, (tok, tok), 1))
        rank = dot(routed.astype(BF16), jnp.where(earlier, 1.0, 0.0).astype(BF16))
        lanes = slice(side * tok, (side + 1) * tok)
        slot_c[pair, :, lanes] = jnp.where(routed > 0.5, rank + float(side * CAP), -float(R))
        wgt_c[pair, :, lanes] = weight

    if LINE:
        routing(e, 0, 0)
    own_rows.wait()
    if LINE:
        start_up(0, 1)

    with jax.named_scope("barrierw"):
        pl.semaphore_wait(barrier, M + has_left.astype(jnp.int32) + has_right.astype(jnp.int32))

    def sent_sem(side, p, s):
        return ag_s.at[side, min(p, 1)] if LINE else ag_s.at[side, p, s]

    def gather_to(s, side, target, parts=(0, 1, 2)):
        copies = []
        for p in parts:
            ref = route.at[s] if p == 0 else xall.at[s, pl.ds((p - 1) * half, half)]
            copies.append(remote(ref, ref, sent_sem(side, p, s), ag_r.at[p, s], expert=target))
        return copies

    def start_right(s, parts=(0, 1, 2)):
        @pl.when(has_right)
        def _():
            for copy in gather_to(s, 0, e + 1, parts):
                copy.start()

    def start_left(s, parts=(0, 1, 2)):
        @pl.when(has_left)
        def _():
            for copy in gather_to(s, 1, e - 1, parts):
                copy.start()

    def gather_step(k, parts=(0, 1, 2)):
        @pl.when(e - k >= 0)
        def _():
            for copy in gather_to(e - k, 0, e, parts):
                copy.wait_recv()
            start_right(e - k, parts)

        @pl.when(e + k <= E - 1)
        def _():
            for copy in gather_to(e + k, 1, e, parts):
                copy.wait_recv()
            start_left(e + k, parts)

    def arrived(s, parts=(0, 1, 2)):
        for copy in gather_to(s, 0, e, parts):
            copy.wait_recv()

    for parts in ((0, 1), (2,)):
        start_right(e, parts)
        start_left(e, parts)

    if not LINE:
        def whole_step(k, carry):
            gather_step(k)
            return carry

        def list_pair(p, carry):
            routing(2 * p, p, 0)
            routing(2 * p + 1, p, 1)
            return carry

        lax.fori_loop(1, E, whole_step, 0)
        lax.fori_loop(0, E // 2, list_pair, 0)

    class Item:
        def __init__(self, j, pos, n, q=0):
            self.j, self.n, self.q = j, n, q
            self.rows, self.toks = n * CAP, n * tok
            self.buf = j * NCH + q
            self.sem = 2 * self.buf + (pos // 2 if isinstance(pos, int) else lax.div(pos, 2))
            start = pos * CAP if isinstance(pos, int) else pl.multiple_of(pos * CAP, n * CAP)
            self.span = pl.ds(start, self.rows)
            first = q * (G // 2) + (pos // 2 if isinstance(pos, int) else lax.div(pos, 2))
            self.pairs = [first + i for i in range(n // 2)]
            if not LINE:
                self.blocks = [q * G + i for i in range(n)]
            elif n == 4:
                self.blocks = order
            else:
                self.blocks = [jnp.where(pos == 0, e, fa), jnp.where(pos == 0, nb, fb)]

        def pieces(self):
            if not LINE or self.n < 4:
                return [self]
            return [Item(self.j, p, n) for p, n in self.cut]

        def row(self, table, step):
            return jnp.concatenate(
                [table[p, pl.ds(self.j, 1), :] + 2 * step * i
                 for i, p in enumerate(self.pairs)], axis=1)

    def taken(it):
        row = it.row(slot_c, float(CAP))
        return (row.astype(jnp.int32)
                == lax.broadcasted_iota(jnp.int32, (it.rows, it.toks), 0))

    def pair_copy(it):
        return remote(s1.at[it.buf, :, it.span], r1.at[it.buf, :, it.span],
                      p_s, p_r.at[it.sem], dp=mate)

    def sum_copy(it, k):
        return remote(s2.at[it.buf, k - 1, it.span], r2.at[it.buf, k - 1, it.span],
                      q_s, q_r.at[it.sem, k - 1], dp=2 * across(k) + c)

    def share_copy(it, k):
        return remote(hid.at[it.buf, d, it.span], hid.at[it.buf, d, it.span],
                      h_s, h_r.at[it.sem, k - 1], dp=2 * across(k) + c)

    def mate_copy(it, k):
        block = 2 * source(k) + c
        return remote(hid.at[it.buf, block, it.span], hid.at[it.buf, block, it.span],
                      h_s, f_r.at[it.sem], dp=mate)

    def stage_a(it, first, last):
        j, span = it.j, it.span
        slot = lax.rem(j, NB)

        pick = jnp.where(taken(it), 1.0, 0.0).astype(BF16)

        @pl.when(first)
        def _():
            for copy in w_gu(j, slot):
                copy.wait()

        for at in range(0, width, ct):
            xq = jnp.concatenate([xall[b, :, at:at + ct] for b in it.blocks], axis=0)
            rows[:it.rows, at:at + ct] = dot(pick, xq).astype(BF16)

        def block(m, core):
            cols = pl.ds(pl.multiple_of((2 * m + core) * hb, hb), hb)
            xr = rows[:it.rows, :]
            return dot(xr, wg[slot, :, cols]), dot(xr, wu[slot, :, cols])

        for m in range(M):
            g, u = block(m, 1 - c)
            s1[it.buf, m, span, :hb] = g.astype(BF16)
            s1[it.buf, m, span, hb:] = u.astype(BF16)
        for piece in it.pieces():
            pair_copy(piece).start()
        for m in range(M):
            g, u = block(m, c)
            keep[it.buf, m, span, :hb] = g.astype(BF16)
            keep[it.buf, m, span, hb:] = u.astype(BF16)

        @pl.when(last & (j + NB < EL))
        def _():
            for copy in w_gu(j + NB, slot):
                copy.start()

    def stage_b(it):
        i, span = it.buf, it.span
        pair_copy(it).wait_recv()
        for k in range(1, M):
            to = across(k)
            s2[i, k - 1, span] = (keep[i, to, span].astype(F32)
                                  + r1[i, to, span].astype(F32)).astype(BF16)
            sum_copy(it, k).start()

    def stage_c(it):
        i, span = it.buf, it.span
        total = keep[i, x, span].astype(F32) + r1[i, x, span].astype(F32)
        for k in range(1, M):
            sum_copy(it, k).wait_recv()
            total = total + r2[i, k - 1, span].astype(F32)
        g, u = total[:, :hb], total[:, hb:]
        hid[i, d, span] = (g / (1.0 + jnp.exp(-g)) * u).astype(BF16)
        for k in range(1, M):
            share_copy(it, k).start()
        mate_copy(it, 0).start()

    def stage_d(it):
        for k in range(1, M):
            share_copy(it, k).wait_recv()
            mate_copy(it, k).start()

    def stage_e(it, first, last):
        j, span = it.j, it.span
        slot = lax.rem(j, ND)
        hit = taken(it)
        scale = jnp.sum(jnp.where(hit, it.row(wgt_c, 0.0), 0.0), axis=1, keepdims=True)
        pick = jnp.where(hit, 1.0, 0.0).astype(BF16)

        @pl.when(first)
        def _():
            w_d(j, slot).wait()

        for piece in it.pieces():
            both = hid.at[it.buf, pl.ds(0, M), piece.span]
            remote(both, both, h_s, f_r.at[piece.sem], dp=mate).wait_recv()
        hidden = jnp.concatenate([hid[it.buf, b, span] for b in range(DP)], axis=1)

        def add_to(at, out):
            add = dot(pick, out, ((0,), (0,)))
            for i, b in enumerate(it.blocks):
                acc[b, :, at:at + ct] += add[i * tok:(i + 1) * tok]

        held = None
        for at in range(0, width, ct):
            out = (dot(hidden, wd[slot, :, at:at + ct]) * scale).astype(BF16)
            if held is not None:
                add_to(*held)
            held = (at, out)
        add_to(*held)

        @pl.when(last & (j + ND < EL))
        def _():
            w_d(j + ND, slot).start()

    def tail(at, s, n, target):
        part = pl.ds(n * half, half)
        return remote(rs_s.at[s, part], rs_in.at[at, part],
                      t_s if LINE else t_s.at[s, n], t_r.at[at, n], expert=target)

    def pass_on(to, s, n, target, have, adds):
        part = pl.ds(n * half, half)

        def alone():
            rs_s[s, part] = acc[s, part].astype(BF16)

        if adds is None:
            alone()
        else:
            pl.when(jnp.logical_not(adds))(alone)

            @pl.when(adds)
            def _():
                tail(have, s, n, e).wait_recv()
                rs_s[s, part] = (acc[s, part] + rs_in[have, part].astype(F32)).astype(BF16)

        tail(to, s, n, target).start()

    if LINE:
        with jax.named_scope("gather1"):
            gather_step(1, (0, 1))
            start_up(*range(2, NB))
            gather_step(1, (2,))
            routing(nb, 0, 1)

        def half_item(t):
            far = (t >= K) & (t < 3 * K)
            j = t - jnp.where(t >= K, K, 0) - jnp.where(t >= 3 * K, K, 0)
            return Item(j, jnp.where(far, 2, 0), 2)

        def full_item(j):
            it = Item(j, 0, 4)
            it.cut = ((2, 2), (0, 2))
            return it

        def run_a(u):
            @pl.when(u < 2 * K)
            def _():
                stage_a(half_item(u), u < K, u >= K)

            @pl.when(u >= 2 * K)
            def _():
                stage_a(full_item(u - K), u >= 0, u >= 0)

        def run_e(u):
            @pl.when(u < K)
            def _():
                stage_e(full_item(u), u >= 0, u >= 0)

            @pl.when(u >= K)
            def _():
                stage_e(half_item(u + K), u < 2 * K, u < 0)

        def event(u):
            for n, parts in enumerate(((0, 1), (2,))):
                @pl.when((u == n) & mid)
                def _(parts=parts):
                    arrived(fb, parts)
                    for copy in gather_to(fb, 1 - onward, 3 - fb, parts):
                        copy.start()

                @pl.when((u == 4 + n) & mid)
                def _(n=n):
                    pass_on(1, fb, n, fb, 0, u >= 0)

            @pl.when(u == 0)
            def _():
                start_down()

            @pl.when(u == 2)
            def _():
                @pl.when(jnp.logical_not(mid))
                def _():
                    arrived(fa)
                    arrived(fb)

                routing(fa, 1, 0)
                routing(fb, 1, 1)

            @pl.when((u == 3) & jnp.logical_not(mid))
            def _():
                for s, to in ((fb, 0), (fa, 2)):
                    for n in range(2):
                        pass_on(to, s, n, nb, None, None)

            @pl.when((u == 3) & mid)
            def _():
                for n in range(2):
                    pass_on(0, fa, n, fa, None, None)

        words = packed(ORDER)

        def light(code):
            for n, stage in enumerate((stage_b, stage_c, stage_d)):
                @pl.when(lax.div(code, 16) == n + 1)
                def _(n=n, stage=stage):
                    with jax.named_scope("BCD"[n]):
                        stage(half_item(lax.rem(code, 16)))

        def heavy(code):
            for n, run in enumerate((run_a, run_e, event)):
                @pl.when(lax.div(code, 16) == n + 1)
                def _(n=n, run=run):
                    with jax.named_scope("AEX"[n]):
                        run(lax.rem(code, 16))

        def step(i, carry):
            word = jnp.int32(words[0])
            for n, value in enumerate(words[1:]):
                word = jnp.where(i == n + 1, value, word)
            for n in range(3):
                code = lax.rem(lax.div(word, 64 ** n), 64)
                pl.when(code > 0)(functools.partial(light, code))
            heavy(lax.div(word, 64 ** 3))
            return carry

        lax.fori_loop(0, len(words), step, 0)

        with jax.named_scope("r2"):
            for n in range(2):
                pass_on(jnp.where(mid, 4, 3), nb, n, nb, 2, mid)
    else:
        stages = (lambda it: stage_a(it, first_of(it), last_of(it)), stage_b, stage_c, stage_d,
                  lambda it: stage_e(it, first_of(it), last_of(it)))

        def first_of(it):
            return it.q == 0

        def last_of(it):
            return it.q == NCH - 1

        def item(t):
            return Item(lax.div(t, NCH), 0, G, lax.rem(t, NCH))

        def step(i, carry):
            for stage, lag in zip(stages, LAGS):
                @pl.when((i >= lag) & (i < N + lag))
                def _(stage=stage, lag=lag):
                    stage(item(i - lag))
            return carry

        lax.fori_loop(0, N + LAGS[-1], step, 0)

        def tail_step(t, carry):
            far, near = E - 1 - t, t
            for n in range(2):
                @pl.when((far > e) & has_right)
                def _(n=n):
                    pass_on(far, far, n, e + 1, far, has_left)

                @pl.when((near < e) & has_left)
                def _(n=n):
                    pass_on(E + near, near, n, e - 1, E + near, has_right)
            return carry

        lax.fori_loop(0, E - 1, tail_step, 0)

    with jax.named_scope("drain"):
        if LINE:
            for side, has, count in ((0, has_right, e + 1), (1, has_left, E - e)):
                for n in range(1, E):
                    @pl.when(has & (count == n))
                    def _(side=side, n=n):
                        for p, ref in enumerate((route, xall)):
                            ref = ref.at[pl.ds(0, n)]
                            remote(ref, ref, ag_s.at[side, p], ag_r.at[p, 0], expert=e).wait_send()
        else:
            def drain_line(s, carry):
                for p in range(3):
                    @pl.when((s <= e) & has_right)
                    def _(p=p):
                        gather_to(s, 0, e, (p,))[0].wait_send()

                    @pl.when((s >= e) & has_left)
                    def _(p=p):
                        gather_to(s, 1, e, (p,))[0].wait_send()
                return carry

            lax.fori_loop(0, E, drain_line, 0)
        remote(s1, r1, p_s, p_r.at[0], dp=mate).wait_send()
        remote(s2, r2, q_s, q_r.at[0, 0], dp=mate).wait_send()
        sent = hid.at[:, pl.ds(0, 2 * M - 1)]
        remote(sent, sent, h_s, h_r.at[0, 0], dp=mate).wait_send()

    with jax.named_scope("own"):
        for n in range(2):
            part = pl.ds(n * half, half)
            if LINE:
                total = acc[e, part]
                for at in (jnp.where(mid, 3, 0), jnp.where(mid, 4, 1)):
                    tail(at, e, n, e).wait_recv()
                    total = total + rs_in[at, part].astype(F32)
                out_ref[part] = total.astype(BF16)
            else:
                for at, has in ((e, has_left), (E + e, has_right)):
                    @pl.when(has)
                    def _(at=at):
                        tail(at, e, n, e).wait_recv()
                        acc[e, part] = acc[e, part] + rs_in[at, part].astype(F32)

                out_ref[part] = acc[e, part].astype(BF16)

        if LINE:
            three = rs_s.at[pl.ds(0, E - 1)]
            remote(three, three, t_s, t_r.at[0, 0], expert=e).wait_send()
        else:
            def drain_sums(s, carry):
                @pl.when(s != e)
                def _():
                    for n in range(2):
                        tail(s, s, n, e).wait_send()
                return carry

            lax.fori_loop(0, E, drain_sums, 0)


def on_device(tokens, expert_ids, scores, w_gate, w_up, w_down):
    E, DP = lax.axis_size("expert"), lax.axis_size("dp")
    tok, width = tokens.shape
    top = expert_ids.shape[1]
    EL, _, H = w_gate.shape
    n_exp = E * EL
    CAP = 2 * tok * top // n_exp
    G = min(E, 4)
    NCH = E // G
    LINE = E == 4 and EL == 8
    NB = EL // 2 if LINE else min(3, EL)
    ND = EL // 2 + 2 if LINE else min(3, EL)
    ct = tile_of(width)
    M, hb, R, N = DP // 2, H // DP, G * CAP, EL * NCH
    EP = max(EL, 8)
    vmem, dma = pltpu.VMEM, pltpu.SemaphoreType.DMA
    scratch = [
        vmem((NB, width, H), BF16), vmem((NB, width, H), BF16), vmem((ND, H, width), BF16),
        vmem((E, tok, width), BF16), vmem((E, 2 * top, tok), F32),
        vmem((E // 2, EP, 2 * tok), F32), vmem((E // 2, EP, 2 * tok), F32),
        vmem((R, width), BF16),
        vmem((N, M, R, 2 * hb), BF16), vmem((N, M, R, 2 * hb), BF16),
        vmem((N, M, R, 2 * hb), BF16),
        vmem((N, M - 1, R, 2 * hb), BF16), vmem((N, M - 1, R, 2 * hb), BF16),
        vmem((N, DP, R, hb), BF16),
        vmem((E, tok, width), F32),
        vmem((E, tok, width), BF16), vmem((5 if LINE else 2 * E, tok, width), BF16),
        vmem((top, tok), jnp.int32), vmem((top, tok), F32),
        dma((3,)), dma((2, NB)), dma((ND,)), dma((2, 2) if LINE else (2, 3, E)), dma((3, E)),
        dma(()), dma((2 * N,)), dma(()), dma((2 * N, M - 1)), dma(()), dma((2 * N, M - 1)),
        dma((2 * N,)),
        dma(() if LINE else (E, 2)), dma((5 if LINE else 2 * E, 2)),
    ]
    whole = pl.BlockSpec(memory_space=pltpu.VMEM)
    hbm = pl.BlockSpec(memory_space=pl.ANY)
    return pl.pallas_call(
        functools.partial(kernel, (E, DP, EL, NCH, G, CAP, NB, ND, LINE, ct)),
        out_shape=pltpu.VMEM((tok, width), BF16),
        in_specs=[hbm] * 6,
        out_specs=whole,
        scratch_shapes=scratch,
        compiler_params=pltpu.CompilerParams(
            collective_id=0, has_side_effects=True, vmem_limit_bytes=62 * 2**20),
        name="routed_experts",
    )(tokens, expert_ids.T, scores.T, w_gate, w_up, w_down)


def solution(mesh):
    in_specs = (
        P(("groups", "expert"), "dp"),
        P(("groups", "expert"), None),
        P(("groups", "expert"), None),
        P("expert", "dp", None),
        P("expert", "dp", None),
        P("expert", None, "dp"),
    )
    out_specs = P(("groups", "expert"), "dp")
    return jax.shard_map(
        on_device, mesh=mesh, in_specs=in_specs, out_specs=out_specs, check_vma=False
    )
```

```python
import functools

import jax
import jax.numpy as jnp
from jax import lax
from jax.experimental import pallas as pl
from jax.experimental.pallas import tpu as pltpu
from jax.sharding import PartitionSpec as P

MESH = pl.DeviceIdType.MESH
F32, BF16 = jnp.float32, jnp.bfloat16
LAGS = (0, 1, 3, 5, 7)
A, E, X = 16, 32, 48
B, C, D = 16, 32, 48
ORDER = (
    (0, 0, 0, A), (0, 0, 0, X), (B, 0, 0, A + 1), (0, 0, 0, X + 1), (B + 1, 0, 0, A + 2),
    (B + 2, C, 0, A + 3), (B + 3, C + 1, 0, X + 2), (0, 0, 0, A + 4), (C + 2, B + 4, 0, A + 5),
    (D, B + 5, C + 3, A + 6), (D + 1, B + 6, C + 4, A + 7), (D + 2, B + 7, 0, A + 8),
    (C + 5, D + 3, B + 8, 0), (C + 6, 0, 0, A + 9), (D + 4, B + 9, 0, A + 10),
    (C + 7, D + 5, B + 10, A + 11), (C + 8, D + 6, B + 11, E), (C + 9, 0, 0, E + 1),
    (D + 7, B + 12, 0, E + 2), (C + 10, 0, 0, E + 3), (D + 8, C + 11, B + 13, 0),
    (D + 9, 0, 0, E + 4), (C + 12, B + 14, D + 10, E + 5), (D + 11, B + 15, 0, E + 6),
    (C + 13, 0, 0, E + 7), (0, 0, 0, X + 3), (C + 14, D + 12, C + 15, 0), (D + 13, 0, 0, E + 8),
    (D + 14, 0, 0, E + 9), (0, 0, 0, X + 4), (D + 15, 0, 0, E + 10), (0, 0, 0, X + 5),
    (0, 0, 0, E + 11),
)


def packed(rows):
    return [a + 64 * (b + 64 * (c + 64 * d)) for a, b, c, d in rows]


def dot(a, b, dims=((1,), (0,))):
    return lax.dot_general(a, b, (dims, ((), ())), preferred_element_type=F32)


def remote(src, dst, send, recv, **where):
    return pltpu.make_async_remote_copy(
        src_ref=src, dst_ref=dst, send_sem=send, recv_sem=recv,
        device_id=where, device_id_type=MESH,
    )


def tile_of(size):
    for tile in (512, 384, 256, 128):
        if size % tile == 0:
            return tile
    return size


def kernel(dims, tok_hbm, ids_hbm, sco_hbm, wg_hbm, wu_hbm, wd_hbm, out_ref,
           wg, wu, wd, xall, route, slot_c, wgt_c, rows, s1, r1, keep, s2, r2, hid, acc,
           rs_s, rs_in, ids_ref, sco_ref,
           io_sem, wsem, dsem, ag_s, ag_r, p_s, p_r, q_s, q_r, h_s, h_r, f_r, t_s, t_r):
    E, DP, EL, NCH, G, CAP, NB, ND, LINE, ct = dims
    M = DP // 2
    tok, width = tok_hbm.shape
    top = ids_hbm.shape[0]
    H = wg.shape[2]
    hb = H // DP
    R, T = G * CAP, G * tok
    N = EL * NCH
    K = EL // 2
    half = tok // 2
    EP = slot_c.shape[1]
    e = lax.axis_index("expert")
    d = lax.axis_index("dp")
    x, c = lax.div(d, 2), lax.rem(d, 2)
    mate = 2 * x + 1 - c
    has_left, has_right = e > 0, e < E - 1
    if LINE:
        low = e < 2
        mid = (e == 1) | (e == 2)
        onward = jnp.where(low, 0, 1)
        nb = jnp.where(low, e + 1, e - 1)
        fb = jnp.where(low, 3, 0)
        fa = 6 - e - nb - fb
        order = (e, nb, fa, fb)

    def across(k):
        return lax.rem(x + k, M)

    def source(k):
        return lax.rem(x + M - k, M)

    def w_gu(j, slot):
        return (pltpu.make_async_copy(wg_hbm.at[j], wg.at[slot], wsem.at[0, slot]),
                pltpu.make_async_copy(wu_hbm.at[j], wu.at[slot], wsem.at[1, slot]))

    def w_d(j, slot):
        return pltpu.make_async_copy(wd_hbm.at[j], wd.at[slot], dsem.at[slot])

    def start_down():
        for j in range(ND):
            w_d(j, j).start()

    own_rows = pltpu.make_async_copy(tok_hbm, xall.at[e], io_sem.at[0])
    own_rows.start()
    own_ids = pltpu.make_async_copy(ids_hbm, ids_ref, io_sem.at[1])
    own_scores = pltpu.make_async_copy(sco_hbm, sco_ref, io_sem.at[2])
    own_ids.start()
    own_scores.start()
    def start_up(*experts):
        for j in experts:
            for copy in w_gu(j, j):
                copy.start()

    if not LINE:
        start_up(*range(NB))
        start_down()

    barrier = pltpu.get_barrier_semaphore()

    @pl.when(has_left)
    def _():
        pl.semaphore_signal(barrier, inc=1, device_id={"expert": e - 1}, device_id_type=MESH)

    @pl.when(has_right)
    def _():
        pl.semaphore_signal(barrier, inc=1, device_id={"expert": e + 1}, device_id_type=MESH)

    pl.semaphore_signal(barrier, inc=1, device_id={"dp": mate}, device_id_type=MESH)
    for k in range(1, M):
        pl.semaphore_signal(
            barrier, inc=1, device_id={"dp": 2 * across(k) + c}, device_id_type=MESH)

    acc[...] = jnp.zeros_like(acc)
    own_ids.wait()
    own_scores.wait()
    route[e, :top] = ids_ref[...].astype(F32)
    route[e, top:] = sco_ref[...]

    def routing(block, pair, side):
        affinity = 1.0 / (1.0 + jnp.exp(-route[block, top:]))
        weights = 2.5 * affinity / jnp.sum(affinity, axis=0, keepdims=True)
        number = lax.broadcasted_iota(jnp.int32, (EP, tok), 0) + e * EL
        number = number.astype(F32)
        routed = jnp.zeros((EP, tok), F32)
        weight = jnp.zeros((EP, tok), F32)
        for k in range(top):
            hit = route[block, k:k + 1] == number
            routed = routed + jnp.where(hit, 1.0, 0.0)
            weight = weight + jnp.where(hit, weights[k:k + 1, :], 0.0)
        earlier = (lax.broadcasted_iota(jnp.int32, (tok, tok), 0)
                   < lax.broadcasted_iota(jnp.int32, (tok, tok), 1))
        rank = dot(routed.astype(BF16), jnp.where(earlier, 1.0, 0.0).astype(BF16))
        lanes = slice(side * tok, (side + 1) * tok)
        slot_c[pair, :, lanes] = jnp.where(routed > 0.5, rank + float(side * CAP), -float(R))
        wgt_c[pair, :, lanes] = weight

    if LINE:
        routing(e, 0, 0)
    own_rows.wait()
    if LINE:
        start_up(0, 1)

    with jax.named_scope("barrierw"):
        pl.semaphore_wait(barrier, M + has_left.astype(jnp.int32) + has_right.astype(jnp.int32))

    def sent_sem(side, p, s):
        return ag_s.at[side, min(p, 1)] if LINE else ag_s.at[side, p, s]

    def gather_to(s, side, target, parts=(0, 1, 2)):
        copies = []
        for p in parts:
            ref = route.at[s] if p == 0 else xall.at[s, pl.ds((p - 1) * half, half)]
            copies.append(remote(ref, ref, sent_sem(side, p, s), ag_r.at[p, s], expert=target))
        return copies

    def start_right(s, parts=(0, 1, 2)):
        @pl.when(has_right)
        def _():
            for copy in gather_to(s, 0, e + 1, parts):
                copy.start()

    def start_left(s, parts=(0, 1, 2)):
        @pl.when(has_left)
        def _():
            for copy in gather_to(s, 1, e - 1, parts):
                copy.start()

    def gather_step(k, parts=(0, 1, 2)):
        @pl.when(e - k >= 0)
        def _():
            for copy in gather_to(e - k, 0, e, parts):
                copy.wait_recv()
            start_right(e - k, parts)

        @pl.when(e + k <= E - 1)
        def _():
            for copy in gather_to(e + k, 1, e, parts):
                copy.wait_recv()
            start_left(e + k, parts)

    def arrived(s, parts=(0, 1, 2)):
        for copy in gather_to(s, 0, e, parts):
            copy.wait_recv()

    for parts in ((0, 1), (2,)):
        start_right(e, parts)
        start_left(e, parts)

    if not LINE:
        def whole_step(k, carry):
            gather_step(k)
            return carry

        def list_pair(p, carry):
            routing(2 * p, p, 0)
            routing(2 * p + 1, p, 1)
            return carry

        lax.fori_loop(1, E, whole_step, 0)
        lax.fori_loop(0, E // 2, list_pair, 0)

    class Item:
        def __init__(self, j, pos, n, q=0):
            self.j, self.n, self.q = j, n, q
            self.rows, self.toks = n * CAP, n * tok
            self.buf = j * NCH + q
            self.sem = 2 * self.buf + (pos // 2 if isinstance(pos, int) else lax.div(pos, 2))
            start = pos * CAP if isinstance(pos, int) else pl.multiple_of(pos * CAP, n * CAP)
            self.span = pl.ds(start, self.rows)
            first = q * (G // 2) + (pos // 2 if isinstance(pos, int) else lax.div(pos, 2))
            self.pairs = [first + i for i in range(n // 2)]
            if not LINE:
                self.blocks = [q * G + i for i in range(n)]
            elif n == 4:
                self.blocks = order
            else:
                self.blocks = [jnp.where(pos == 0, e, fa), jnp.where(pos == 0, nb, fb)]

        def pieces(self):
            if not LINE or self.n < 4:
                return [self]
            return [Item(self.j, p, n) for p, n in self.cut]

        def row(self, table, step):
            return jnp.concatenate(
                [table[p, pl.ds(self.j, 1), :] + 2 * step * i
                 for i, p in enumerate(self.pairs)], axis=1)

    def taken(it):
        row = it.row(slot_c, float(CAP))
        return (row.astype(jnp.int32)
                == lax.broadcasted_iota(jnp.int32, (it.rows, it.toks), 0))

    def pair_copy(it):
        return remote(s1.at[it.buf, :, it.span], r1.at[it.buf, :, it.span],
                      p_s, p_r.at[it.sem], dp=mate)

    def sum_copy(it, k):
        return remote(s2.at[it.buf, k - 1, it.span], r2.at[it.buf, k - 1, it.span],
                      q_s, q_r.at[it.sem, k - 1], dp=2 * across(k) + c)

    def share_copy(it, k):
        return remote(hid.at[it.buf, d, it.span], hid.at[it.buf, d, it.span],
                      h_s, h_r.at[it.sem, k - 1], dp=2 * across(k) + c)

    def mate_copy(it, k):
        block = 2 * source(k) + c
        return remote(hid.at[it.buf, block, it.span], hid.at[it.buf, block, it.span],
                      h_s, f_r.at[it.sem], dp=mate)

    def stage_a(it, first, last):
        j, span = it.j, it.span
        slot = lax.rem(j, NB)

        pick = jnp.where(taken(it), 1.0, 0.0).astype(BF16)

        @pl.when(first)
        def _():
            for copy in w_gu(j, slot):
                copy.wait()

        for at in range(0, width, ct):
            xq = jnp.concatenate([xall[b, :, at:at + ct] for b in it.blocks], axis=0)
            rows[:it.rows, at:at + ct] = dot(pick, xq).astype(BF16)

        def block(m, core):
            cols = pl.ds(pl.multiple_of((2 * m + core) * hb, hb), hb)
            xr = rows[:it.rows, :]
            return dot(xr, wg[slot, :, cols]), dot(xr, wu[slot, :, cols])

        for m in range(M):
            g, u = block(m, 1 - c)
            s1[it.buf, m, span, :hb] = g.astype(BF16)
            s1[it.buf, m, span, hb:] = u.astype(BF16)
        for piece in it.pieces():
            pair_copy(piece).start()
        for m in range(M):
            g, u = block(m, c)
            keep[it.buf, m, span, :hb] = g.astype(BF16)
            keep[it.buf, m, span, hb:] = u.astype(BF16)

        @pl.when(last & (j + NB < EL))
        def _():
            for copy in w_gu(j + NB, slot):
                copy.start()

    def stage_b(it):
        i, span = it.buf, it.span
        pair_copy(it).wait_recv()
        for k in range(1, M):
            to = across(k)
            s2[i, k - 1, span] = (keep[i, to, span].astype(F32)
                                  + r1[i, to, span].astype(F32)).astype(BF16)
            sum_copy(it, k).start()

    def stage_c(it):
        i, span = it.buf, it.span
        total = keep[i, x, span].astype(F32) + r1[i, x, span].astype(F32)
        for k in range(1, M):
            sum_copy(it, k).wait_recv()
            total = total + r2[i, k - 1, span].astype(F32)
        g, u = total[:, :hb], total[:, hb:]
        hid[i, d, span] = (g / (1.0 + jnp.exp(-g)) * u).astype(BF16)
        for k in range(1, M):
            share_copy(it, k).start()
        mate_copy(it, 0).start()

    def stage_d(it):
        for k in range(1, M):
            share_copy(it, k).wait_recv()
            mate_copy(it, k).start()

    def stage_e(it, first, last):
        j, span = it.j, it.span
        slot = lax.rem(j, ND)
        hit = taken(it)
        scale = jnp.sum(jnp.where(hit, it.row(wgt_c, 0.0), 0.0), axis=1, keepdims=True)
        pick = jnp.where(hit, 1.0, 0.0).astype(BF16)

        @pl.when(first)
        def _():
            w_d(j, slot).wait()

        for piece in it.pieces():
            both = hid.at[it.buf, pl.ds(0, M), piece.span]
            remote(both, both, h_s, f_r.at[piece.sem], dp=mate).wait_recv()
        hidden = jnp.concatenate([hid[it.buf, b, span] for b in range(DP)], axis=1)

        def add_to(at, out):
            add = dot(pick, out, ((0,), (0,)))
            for i, b in enumerate(it.blocks):
                acc[b, :, at:at + ct] += add[i * tok:(i + 1) * tok]

        held = None
        for at in range(0, width, ct):
            out = (dot(hidden, wd[slot, :, at:at + ct]) * scale).astype(BF16)
            if held is not None:
                add_to(*held)
            held = (at, out)
        add_to(*held)

        @pl.when(last & (j + ND < EL))
        def _():
            w_d(j + ND, slot).start()

    def tail(at, s, n, target):
        part = pl.ds(n * half, half)
        return remote(rs_s.at[s, part], rs_in.at[at, part],
                      t_s if LINE else t_s.at[s, n], t_r.at[at, n], expert=target)

    def pass_on(to, s, n, target, have, adds):
        part = pl.ds(n * half, half)

        def alone():
            rs_s[s, part] = acc[s, part].astype(BF16)

        if adds is None:
            alone()
        else:
            pl.when(jnp.logical_not(adds))(alone)

            @pl.when(adds)
            def _():
                tail(have, s, n, e).wait_recv()
                rs_s[s, part] = (acc[s, part] + rs_in[have, part].astype(F32)).astype(BF16)

        tail(to, s, n, target).start()

    if LINE:
        with jax.named_scope("gather1"):
            gather_step(1, (0, 1))
            start_up(*range(2, NB))
            gather_step(1, (2,))
            routing(nb, 0, 1)

        def half_item(t):
            far = (t >= K) & (t < 3 * K)
            j = t - jnp.where(t >= K, K, 0) - jnp.where(t >= 3 * K, K, 0)
            return Item(j, jnp.where(far, 2, 0), 2)

        def full_item(j):
            it = Item(j, 0, 4)
            it.cut = ((2, 2), (0, 2))
            return it

        def run_a(u):
            @pl.when(u < 2 * K)
            def _():
                stage_a(half_item(u), u < K, u >= K)

            @pl.when(u >= 2 * K)
            def _():
                stage_a(full_item(u - K), u >= 0, u >= 0)

        def run_e(u):
            @pl.when(u < K)
            def _():
                stage_e(full_item(u), u >= 0, u >= 0)

            @pl.when(u >= K)
            def _():
                stage_e(half_item(u + K), u < 2 * K, u < 0)

        def event(u):
            for n, parts in enumerate(((0, 1), (2,))):
                @pl.when((u == n) & mid)
                def _(parts=parts):
                    arrived(fb, parts)
                    for copy in gather_to(fb, 1 - onward, 3 - fb, parts):
                        copy.start()

                @pl.when((u == 4 + n) & mid)
                def _(n=n):
                    pass_on(1, fb, n, fb, 0, u >= 0)

            @pl.when(u == 0)
            def _():
                start_down()

            @pl.when(u == 2)
            def _():
                @pl.when(jnp.logical_not(mid))
                def _():
                    arrived(fa)
                    arrived(fb)

                routing(fa, 1, 0)
                routing(fb, 1, 1)

            @pl.when((u == 3) & jnp.logical_not(mid))
            def _():
                for s, to in ((fb, 0), (fa, 2)):
                    for n in range(2):
                        pass_on(to, s, n, nb, None, None)

            @pl.when((u == 3) & mid)
            def _():
                for n in range(2):
                    pass_on(0, fa, n, fa, None, None)

        words = packed(ORDER)

        def light(code):
            for n, stage in enumerate((stage_b, stage_c, stage_d)):
                @pl.when(lax.div(code, 16) == n + 1)
                def _(n=n, stage=stage):
                    with jax.named_scope("BCD"[n]):
                        stage(half_item(lax.rem(code, 16)))

        def heavy(code):
            for n, run in enumerate((run_a, run_e, event)):
                @pl.when(lax.div(code, 16) == n + 1)
                def _(n=n, run=run):
                    with jax.named_scope("AEX"[n]):
                        run(lax.rem(code, 16))

        def step(i, carry):
            word = jnp.int32(words[0])
            for n, value in enumerate(words[1:]):
                word = jnp.where(i == n + 1, value, word)
            for n in range(3):
                code = lax.rem(lax.div(word, 64 ** n), 64)
                pl.when(code > 0)(functools.partial(light, code))
            heavy(lax.div(word, 64 ** 3))
            return carry

        lax.fori_loop(0, len(words), step, 0)

        with jax.named_scope("r2"):
            for n in range(2):
                pass_on(jnp.where(mid, 4, 3), nb, n, nb, 2, mid)
    else:
        stages = (lambda it: stage_a(it, first_of(it), last_of(it)), stage_b, stage_c, stage_d,
                  lambda it: stage_e(it, first_of(it), last_of(it)))

        def first_of(it):
            return it.q == 0

        def last_of(it):
            return it.q == NCH - 1

        def item(t):
            return Item(lax.div(t, NCH), 0, G, lax.rem(t, NCH))

        def step(i, carry):
            for stage, lag in zip(stages, LAGS):
                @pl.when((i >= lag) & (i < N + lag))
                def _(stage=stage, lag=lag):
                    stage(item(i - lag))
            return carry

        lax.fori_loop(0, N + LAGS[-1], step, 0)

        def tail_step(t, carry):
            far, near = E - 1 - t, t
            for n in range(2):
                @pl.when((far > e) & has_right)
                def _(n=n):
                    pass_on(far, far, n, e + 1, far, has_left)

                @pl.when((near < e) & has_left)
                def _(n=n):
                    pass_on(E + near, near, n, e - 1, E + near, has_right)
            return carry

        lax.fori_loop(0, E - 1, tail_step, 0)

    with jax.named_scope("drain"):
        if LINE:
            for side, has, count in ((0, has_right, e + 1), (1, has_left, E - e)):
                for n in range(1, E):
                    @pl.when(has & (count == n))
                    def _(side=side, n=n):
                        for p, ref in enumerate((route, xall)):
                            ref = ref.at[pl.ds(0, n)]
                            remote(ref, ref, ag_s.at[side, p], ag_r.at[p, 0], expert=e).wait_send()
        else:
            def drain_line(s, carry):
                for p in range(3):
                    @pl.when((s <= e) & has_right)
                    def _(p=p):
                        gather_to(s, 0, e, (p,))[0].wait_send()

                    @pl.when((s >= e) & has_left)
                    def _(p=p):
                        gather_to(s, 1, e, (p,))[0].wait_send()
                return carry

            lax.fori_loop(0, E, drain_line, 0)
        remote(s1, r1, p_s, p_r.at[0], dp=mate).wait_send()
        remote(s2, r2, q_s, q_r.at[0, 0], dp=mate).wait_send()
        sent = hid.at[:, pl.ds(0, 2 * M - 1)]
        remote(sent, sent, h_s, h_r.at[0, 0], dp=mate).wait_send()

    with jax.named_scope("own"):
        for n in range(2):
            part = pl.ds(n * half, half)
            if LINE:
                total = acc[e, part]
                for at in (jnp.where(mid, 3, 0), jnp.where(mid, 4, 1)):
                    tail(at, e, n, e).wait_recv()
                    total = total + rs_in[at, part].astype(F32)
                out_ref[part] = total.astype(BF16)
            else:
                for at, has in ((e, has_left), (E + e, has_right)):
                    @pl.when(has)
                    def _(at=at):
                        tail(at, e, n, e).wait_recv()
                        acc[e, part] = acc[e, part] + rs_in[at, part].astype(F32)

                out_ref[part] = acc[e, part].astype(BF16)

        if LINE:
            three = rs_s.at[pl.ds(0, E - 1)]
            remote(three, three, t_s, t_r.at[0, 0], expert=e).wait_send()
        else:
            def drain_sums(s, carry):
                @pl.when(s != e)
                def _():
                    for n in range(2):
                        tail(s, s, n, e).wait_send()
                return carry

            lax.fori_loop(0, E, drain_sums, 0)


def on_device(tokens, expert_ids, scores, w_gate, w_up, w_down):
    E, DP = lax.axis_size("expert"), lax.axis_size("dp")
    tok, width = tokens.shape
    top = expert_ids.shape[1]
    EL, _, H = w_gate.shape
    n_exp = E * EL
    CAP = 2 * tok * top // n_exp
    G = min(E, 4)
    NCH = E // G
    LINE = E == 4 and EL == 8
    NB = EL // 2 if LINE else min(3, EL)
    ND = EL // 2 + 2 if LINE else min(3, EL)
    ct = tile_of(width)
    M, hb, R, N = DP // 2, H // DP, G * CAP, EL * NCH
    EP = max(EL, 8)
    vmem, dma = pltpu.VMEM, pltpu.SemaphoreType.DMA
    scratch = [
        vmem((NB, width, H), BF16), vmem((NB, width, H), BF16), vmem((ND, H, width), BF16),
        vmem((E, tok, width), BF16), vmem((E, 2 * top, tok), F32),
        vmem((E // 2, EP, 2 * tok), F32), vmem((E // 2, EP, 2 * tok), F32),
        vmem((R, width), BF16),
        vmem((N, M, R, 2 * hb), BF16), vmem((N, M, R, 2 * hb), BF16),
        vmem((N, M, R, 2 * hb), BF16),
        vmem((N, M - 1, R, 2 * hb), BF16), vmem((N, M - 1, R, 2 * hb), BF16),
        vmem((N, DP, R, hb), BF16),
        vmem((E, tok, width), F32),
        vmem((E, tok, width), BF16), vmem((5 if LINE else 2 * E, tok, width), BF16),
        vmem((top, tok), jnp.int32), vmem((top, tok), F32),
        dma((3,)), dma((2, NB)), dma((ND,)), dma((2, 2) if LINE else (2, 3, E)), dma((3, E)),
        dma(()), dma((2 * N,)), dma(()), dma((2 * N, M - 1)), dma(()), dma((2 * N, M - 1)),
        dma((2 * N,)),
        dma(() if LINE else (E, 2)), dma((5 if LINE else 2 * E, 2)),
    ]
    whole = pl.BlockSpec(memory_space=pltpu.VMEM)
    hbm = pl.BlockSpec(memory_space=pl.ANY)
    return pl.pallas_call(
        functools.partial(kernel, (E, DP, EL, NCH, G, CAP, NB, ND, LINE, ct)),
        out_shape=pltpu.VMEM((tok, width), BF16),
        in_specs=[hbm] * 6,
        out_specs=whole,
        scratch_shapes=scratch,
        compiler_params=pltpu.CompilerParams(
            collective_id=0, has_side_effects=True, vmem_limit_bytes=62 * 2**20),
        name="routed_experts",
    )(tokens, expert_ids.T, scores.T, w_gate, w_up, w_down)


def solution(mesh):
    in_specs = (
        P(("groups", "expert"), "dp"),
        P(("groups", "expert"), None),
        P(("groups", "expert"), None),
        P("expert", "dp", None),
        P("expert", "dp", None),
        P("expert", None, "dp"),
    )
    out_specs = P(("groups", "expert"), "dp")
    return jax.shard_map(
        on_device, mesh=mesh, in_specs=in_specs, out_specs=out_specs, check_vma=False
    )
```

```python
import functools

import jax
import jax.numpy as jnp
from jax import lax
from jax.experimental import pallas as pl
from jax.experimental.pallas import tpu as pltpu
from jax.sharding import PartitionSpec as P

MESH = pl.DeviceIdType.MESH
F32, BF16 = jnp.float32, jnp.bfloat16
LAGS = (0, 1, 3, 5, 7)
A, E, X = 16, 32, 48
B, C, D = 16, 32, 48
ORDER = (
    (0, 0, 0, A), (0, 0, 0, X), (B, 0, 0, A + 1), (0, 0, 0, X + 1), (B + 1, 0, 0, A + 2),
    (B + 2, C, 0, A + 3), (B + 3, C + 1, 0, X + 2), (0, 0, 0, A + 4), (C + 2, B + 4, 0, A + 5),
    (D, B + 5, C + 3, A + 6), (D + 1, B + 6, C + 4, A + 7), (D + 2, B + 7, 0, A + 8),
    (C + 5, D + 3, B + 8, 0), (C + 6, 0, 0, A + 9), (D + 4, B + 9, 0, A + 10),
    (C + 7, D + 5, B + 10, A + 11), (C + 8, D + 6, B + 11, E), (C + 9, 0, 0, E + 1),
    (D + 7, B + 12, 0, E + 2), (C + 10, 0, 0, E + 3), (D + 8, C + 11, B + 13, 0),
    (D + 9, 0, 0, E + 4), (C + 12, B + 14, D + 10, E + 5), (D + 11, B + 15, 0, E + 6),
    (C + 13, 0, 0, E + 7), (0, 0, 0, X + 3), (C + 14, D + 12, C + 15, 0), (D + 13, 0, 0, E + 8),
    (D + 14, 0, 0, E + 9), (0, 0, 0, X + 4), (D + 15, 0, 0, E + 10), (0, 0, 0, X + 5),
    (0, 0, 0, E + 11),
)


def packed(rows):
    return [a + 64 * (b + 64 * (c + 64 * d)) for a, b, c, d in rows]


def dot(a, b, dims=((1,), (0,))):
    return lax.dot_general(a, b, (dims, ((), ())), preferred_element_type=F32)


def remote(src, dst, send, recv, **where):
    return pltpu.make_async_remote_copy(
        src_ref=src, dst_ref=dst, send_sem=send, recv_sem=recv,
        device_id=where, device_id_type=MESH,
    )


def tile_of(size):
    for tile in (512, 384, 256, 128):
        if size % tile == 0:
            return tile
    return size


def kernel(dims, tok_hbm, ids_hbm, sco_hbm, wg_hbm, wu_hbm, wd_hbm, out_ref,
           wg, wu, wd, xall, route, slot_c, wgt_c, rows, s1, r1, keep, s2, r2, hid, acc,
           rs_s, rs_in, ids_ref, sco_ref,
           io_sem, wsem, dsem, ag_s, ag_r, p_s, p_r, q_s, q_r, h_s, h_r, f_r, t_s, t_r):
    E, DP, EL, NCH, G, CAP, NB, ND, LINE, ct = dims
    M = DP // 2
    tok, width = tok_hbm.shape
    top = ids_hbm.shape[0]
    H = wg.shape[2]
    hb = H // DP
    R, T = G * CAP, G * tok
    N = EL * NCH
    K = EL // 2
    half = tok // 2
    EP = slot_c.shape[1]
    e = lax.axis_index("expert")
    d = lax.axis_index("dp")
    x, c = lax.div(d, 2), lax.rem(d, 2)
    mate = 2 * x + 1 - c
    has_left, has_right = e > 0, e < E - 1
    if LINE:
        low = e < 2
        mid = (e == 1) | (e == 2)
        onward = jnp.where(low, 0, 1)
        nb = jnp.where(low, e + 1, e - 1)
        fb = jnp.where(low, 3, 0)
        fa = 6 - e - nb - fb
        order = (e, nb, fa, fb)

    def across(k):
        return lax.rem(x + k, M)

    def source(k):
        return lax.rem(x + M - k, M)

    def w_gu(j, slot):
        return (pltpu.make_async_copy(wg_hbm.at[j], wg.at[slot], wsem.at[0, slot]),
                pltpu.make_async_copy(wu_hbm.at[j], wu.at[slot], wsem.at[1, slot]))

    def w_d(j, slot):
        return pltpu.make_async_copy(wd_hbm.at[j], wd.at[slot], dsem.at[slot])

    def start_down():
        for j in range(ND):
            w_d(j, j).start()

    own_rows = pltpu.make_async_copy(tok_hbm, xall.at[e], io_sem.at[0])
    own_rows.start()
    own_ids = pltpu.make_async_copy(ids_hbm, ids_ref, io_sem.at[1])
    own_scores = pltpu.make_async_copy(sco_hbm, sco_ref, io_sem.at[2])
    own_ids.start()
    own_scores.start()
    def start_up(*experts):
        for j in experts:
            for copy in w_gu(j, j):
                copy.start()

    if not LINE:
        start_up(*range(NB))
        start_down()

    barrier = pltpu.get_barrier_semaphore()

    @pl.when(has_left)
    def _():
        pl.semaphore_signal(barrier, inc=1, device_id={"expert": e - 1}, device_id_type=MESH)

    @pl.when(has_right)
    def _():
        pl.semaphore_signal(barrier, inc=1, device_id={"expert": e + 1}, device_id_type=MESH)

    pl.semaphore_signal(barrier, inc=1, device_id={"dp": mate}, device_id_type=MESH)
    for k in range(1, M):
        pl.semaphore_signal(
            barrier, inc=1, device_id={"dp": 2 * across(k) + c}, device_id_type=MESH)

    acc[...] = jnp.zeros_like(acc)
    own_ids.wait()
    own_scores.wait()
    route[e, :top] = ids_ref[...].astype(F32)
    route[e, top:] = sco_ref[...]

    def routing(block, pair, side):
        affinity = 1.0 / (1.0 + jnp.exp(-route[block, top:]))
        weights = 2.5 * affinity / jnp.sum(affinity, axis=0, keepdims=True)
        number = lax.broadcasted_iota(jnp.int32, (EP, tok), 0) + e * EL
        number = number.astype(F32)
        routed = jnp.zeros((EP, tok), F32)
        weight = jnp.zeros((EP, tok), F32)
        for k in range(top):
            hit = route[block, k:k + 1] == number
            routed = routed + jnp.where(hit, 1.0, 0.0)
            weight = weight + jnp.where(hit, weights[k:k + 1, :], 0.0)
        earlier = (lax.broadcasted_iota(jnp.int32, (tok, tok), 0)
                   < lax.broadcasted_iota(jnp.int32, (tok, tok), 1))
        rank = dot(routed.astype(BF16), jnp.where(earlier, 1.0, 0.0).astype(BF16))
        lanes = slice(side * tok, (side + 1) * tok)
        slot_c[pair, :, lanes] = jnp.where(routed > 0.5, rank + float(side * CAP), -float(R))
        wgt_c[pair, :, lanes] = weight

    if LINE:
        routing(e, 0, 0)
    own_rows.wait()
    if LINE:
        start_up(0, 1)

    with jax.named_scope("barrierw"):
        pl.semaphore_wait(barrier, M + has_left.astype(jnp.int32) + has_right.astype(jnp.int32))

    def sent_sem(side, p, s):
        return ag_s.at[side, min(p, 1)] if LINE else ag_s.at[side, p, s]

    def gather_to(s, side, target, parts=(0, 1, 2)):
        copies = []
        for p in parts:
            ref = route.at[s] if p == 0 else xall.at[s, pl.ds((p - 1) * half, half)]
            copies.append(remote(ref, ref, sent_sem(side, p, s), ag_r.at[p, s], expert=target))
        return copies

    def start_right(s, parts=(0, 1, 2)):
        @pl.when(has_right)
        def _():
            for copy in gather_to(s, 0, e + 1, parts):
                copy.start()

    def start_left(s, parts=(0, 1, 2)):
        @pl.when(has_left)
        def _():
            for copy in gather_to(s, 1, e - 1, parts):
                copy.start()

    def gather_step(k, parts=(0, 1, 2)):
        @pl.when(e - k >= 0)
        def _():
            for copy in gather_to(e - k, 0, e, parts):
                copy.wait_recv()
            start_right(e - k, parts)

        @pl.when(e + k <= E - 1)
        def _():
            for copy in gather_to(e + k, 1, e, parts):
                copy.wait_recv()
            start_left(e + k, parts)

    def arrived(s, parts=(0, 1, 2)):
        for copy in gather_to(s, 0, e, parts):
            copy.wait_recv()

    for parts in ((0, 1), (2,)):
        start_right(e, parts)
        start_left(e, parts)

    if not LINE:
        def whole_step(k, carry):
            gather_step(k)
            return carry

        def list_pair(p, carry):
            routing(2 * p, p, 0)
            routing(2 * p + 1, p, 1)
            return carry

        lax.fori_loop(1, E, whole_step, 0)
        lax.fori_loop(0, E // 2, list_pair, 0)

    class Item:
        def __init__(self, j, pos, n, q=0):
            self.j, self.n, self.q = j, n, q
            self.rows, self.toks = n * CAP, n * tok
            self.buf = j * NCH + q
            self.sem = 2 * self.buf + (pos // 2 if isinstance(pos, int) else lax.div(pos, 2))
            self.ring = lax.rem(j + 2 * pos, EL) if LINE else self.sem
            start = pos * CAP if isinstance(pos, int) else pl.multiple_of(pos * CAP, n * CAP)
            self.span = pl.ds(start, self.rows)
            first = q * (G // 2) + (pos // 2 if isinstance(pos, int) else lax.div(pos, 2))
            self.pairs = [first + i for i in range(n // 2)]
            if not LINE:
                self.blocks = [q * G + i for i in range(n)]
            elif n == 4:
                self.blocks = order
            else:
                self.blocks = [jnp.where(pos == 0, e, fa), jnp.where(pos == 0, nb, fb)]

        def pieces(self):
            if not LINE or self.n < 4:
                return [self]
            return [Item(self.j, p, n) for p, n in self.cut]

        def row(self, table, step):
            return jnp.concatenate(
                [table[p, pl.ds(self.j, 1), :] + 2 * step * i
                 for i, p in enumerate(self.pairs)], axis=1)

    def taken(it):
        row = it.row(slot_c, float(CAP))
        return (row.astype(jnp.int32)
                == lax.broadcasted_iota(jnp.int32, (it.rows, it.toks), 0))

    def pair_copy(it):
        return remote(s1.at[it.buf, :, it.span], r1.at[it.buf, :, it.span],
                      p_s, p_r.at[it.ring], dp=mate)

    def sum_copy(it, k):
        return remote(s2.at[it.buf, k - 1, it.span], r2.at[it.buf, k - 1, it.span],
                      q_s, q_r.at[it.ring, k - 1], dp=2 * across(k) + c)

    def share_copy(it, k):
        return remote(hid.at[it.buf, d, it.span], hid.at[it.buf, d, it.span],
                      h_s, h_r.at[it.ring, k - 1], dp=2 * across(k) + c)

    def mate_copy(it, k):
        block = 2 * source(k) + c
        return remote(hid.at[it.buf, block, it.span], hid.at[it.buf, block, it.span],
                      h_s, f_r.at[it.sem], dp=mate)

    def stage_a(it, first, last):
        j, span = it.j, it.span
        slot = lax.rem(j, NB)

        pick = jnp.where(taken(it), 1.0, 0.0).astype(BF16)

        @pl.when(first)
        def _():
            for copy in w_gu(j, slot):
                copy.wait()

        for at in range(0, width, ct):
            xq = jnp.concatenate([xall[b, :, at:at + ct] for b in it.blocks], axis=0)
            rows[:it.rows, at:at + ct] = dot(pick, xq).astype(BF16)

        def block(m, core):
            cols = pl.ds(pl.multiple_of((2 * m + core) * hb, hb), hb)
            xr = rows[:it.rows, :]
            return dot(xr, wg[slot, :, cols]), dot(xr, wu[slot, :, cols])

        for m in range(M):
            g, u = block(m, 1 - c)
            s1[it.buf, m, span, :hb] = g.astype(BF16)
            s1[it.buf, m, span, hb:] = u.astype(BF16)
        for piece in it.pieces():
            pair_copy(piece).start()
        for m in range(M):
            g, u = block(m, c)
            keep[it.buf, m, span, :hb] = g.astype(BF16)
            keep[it.buf, m, span, hb:] = u.astype(BF16)

        @pl.when(last & (j + NB < EL))
        def _():
            for copy in w_gu(j + NB, slot):
                copy.start()

    def stage_b(it):
        i, span = it.buf, it.span
        pair_copy(it).wait_recv()
        for k in range(1, M):
            to = across(k)
            s2[i, k - 1, span] = (keep[i, to, span].astype(F32)
                                  + r1[i, to, span].astype(F32)).astype(BF16)
            sum_copy(it, k).start()

    def stage_c(it):
        i, span = it.buf, it.span
        total = keep[i, x, span].astype(F32) + r1[i, x, span].astype(F32)
        for k in range(1, M):
            sum_copy(it, k).wait_recv()
            total = total + r2[i, k - 1, span].astype(F32)
        g, u = total[:, :hb], total[:, hb:]
        hid[i, d, span] = (g / (1.0 + jnp.exp(-g)) * u).astype(BF16)
        for k in range(1, M):
            share_copy(it, k).start()
        mate_copy(it, 0).start()

    def stage_d(it):
        for k in range(1, M):
            share_copy(it, k).wait_recv()
            mate_copy(it, k).start()

    def stage_e(it, first, last):
        j, span = it.j, it.span
        slot = lax.rem(j, ND)
        hit = taken(it)
        scale = jnp.sum(jnp.where(hit, it.row(wgt_c, 0.0), 0.0), axis=1, keepdims=True)
        pick = jnp.where(hit, 1.0, 0.0).astype(BF16)

        @pl.when(first)
        def _():
            w_d(j, slot).wait()

        for piece in it.pieces():
            both = hid.at[it.buf, pl.ds(0, M), piece.span]
            remote(both, both, h_s, f_r.at[piece.sem], dp=mate).wait_recv()
        hidden = jnp.concatenate([hid[it.buf, b, span] for b in range(DP)], axis=1)

        def add_to(at, out):
            add = dot(pick, out, ((0,), (0,)))
            for i, b in enumerate(it.blocks):
                acc[b, :, at:at + ct] += add[i * tok:(i + 1) * tok]

        held = None
        for at in range(0, width, ct):
            out = (dot(hidden, wd[slot, :, at:at + ct]) * scale).astype(BF16)
            if held is not None:
                add_to(*held)
            held = (at, out)
        add_to(*held)

        @pl.when(last & (j + ND < EL))
        def _():
            w_d(j + ND, slot).start()

    def tail(at, s, n, target):
        part = pl.ds(n * half, half)
        return remote(rs_s.at[s, part], rs_in.at[at, part],
                      t_s if LINE else t_s.at[s, n], t_r.at[at, n], expert=target)

    def pass_on(to, s, n, target, have, adds):
        part = pl.ds(n * half, half)

        def alone():
            rs_s[s, part] = acc[s, part].astype(BF16)

        if adds is None:
            alone()
        else:
            pl.when(jnp.logical_not(adds))(alone)

            @pl.when(adds)
            def _():
                tail(have, s, n, e).wait_recv()
                rs_s[s, part] = (acc[s, part] + rs_in[have, part].astype(F32)).astype(BF16)

        tail(to, s, n, target).start()

    if LINE:
        with jax.named_scope("gather1"):
            gather_step(1, (0, 1))
            start_up(*range(2, NB))
            gather_step(1, (2,))
            routing(nb, 0, 1)

        def half_item(t):
            far = (t >= K) & (t < 3 * K)
            j = t - jnp.where(t >= K, K, 0) - jnp.where(t >= 3 * K, K, 0)
            return Item(j, jnp.where(far, 2, 0), 2)

        def full_item(j):
            it = Item(j, 0, 4)
            it.cut = ((2, 2), (0, 2))
            return it

        def run_a(u):
            @pl.when(u < 2 * K)
            def _():
                stage_a(half_item(u), u < K, u >= K)

            @pl.when(u >= 2 * K)
            def _():
                stage_a(full_item(u - K), u >= 0, u >= 0)

        def run_e(u):
            @pl.when(u < K)
            def _():
                stage_e(full_item(u), u >= 0, u >= 0)

            @pl.when(u >= K)
            def _():
                stage_e(half_item(u + K), u < 2 * K, u < 0)

        def event(u):
            for n, parts in enumerate(((0, 1), (2,))):
                @pl.when((u == n) & mid)
                def _(parts=parts):
                    arrived(fb, parts)
                    for copy in gather_to(fb, 1 - onward, 3 - fb, parts):
                        copy.start()

                @pl.when((u == 4 + n) & mid)
                def _(n=n):
                    pass_on(1, fb, n, fb, 0, u >= 0)

            @pl.when(u == 0)
            def _():
                start_down()

            @pl.when(u == 2)
            def _():
                @pl.when(jnp.logical_not(mid))
                def _():
                    arrived(fa)
                    arrived(fb)

                routing(fa, 1, 0)
                routing(fb, 1, 1)

            @pl.when((u == 3) & jnp.logical_not(mid))
            def _():
                for s, to in ((fb, 0), (fa, 2)):
                    for n in range(2):
                        pass_on(to, s, n, nb, None, None)

            @pl.when((u == 3) & mid)
            def _():
                for n in range(2):
                    pass_on(0, fa, n, fa, None, None)

        words = packed(ORDER)

        def light(code):
            for n, stage in enumerate((stage_b, stage_c, stage_d)):
                @pl.when(lax.div(code, 16) == n + 1)
                def _(n=n, stage=stage):
                    with jax.named_scope("BCD"[n]):
                        stage(half_item(lax.rem(code, 16)))

        def heavy(code):
            for n, run in enumerate((run_a, run_e, event)):
                @pl.when(lax.div(code, 16) == n + 1)
                def _(n=n, run=run):
                    with jax.named_scope("AEX"[n]):
                        run(lax.rem(code, 16))

        def step(i, carry):
            word = jnp.int32(words[0])
            for n, value in enumerate(words[1:]):
                word = jnp.where(i == n + 1, value, word)
            for n in range(3):
                code = lax.rem(lax.div(word, 64 ** n), 64)
                pl.when(code > 0)(functools.partial(light, code))
            heavy(lax.div(word, 64 ** 3))
            return carry

        lax.fori_loop(0, len(words), step, 0)

        with jax.named_scope("r2"):
            for n in range(2):
                pass_on(jnp.where(mid, 4, 3), nb, n, nb, 2, mid)
    else:
        stages = (lambda it: stage_a(it, first_of(it), last_of(it)), stage_b, stage_c, stage_d,
                  lambda it: stage_e(it, first_of(it), last_of(it)))

        def first_of(it):
            return it.q == 0

        def last_of(it):
            return it.q == NCH - 1

        def item(t):
            return Item(lax.div(t, NCH), 0, G, lax.rem(t, NCH))

        def step(i, carry):
            for stage, lag in zip(stages, LAGS):
                @pl.when((i >= lag) & (i < N + lag))
                def _(stage=stage, lag=lag):
                    stage(item(i - lag))
            return carry

        lax.fori_loop(0, N + LAGS[-1], step, 0)

        def tail_step(t, carry):
            far, near = E - 1 - t, t
            for n in range(2):
                @pl.when((far > e) & has_right)
                def _(n=n):
                    pass_on(far, far, n, e + 1, far, has_left)

                @pl.when((near < e) & has_left)
                def _(n=n):
                    pass_on(E + near, near, n, e - 1, E + near, has_right)
            return carry

        lax.fori_loop(0, E - 1, tail_step, 0)

    with jax.named_scope("drain"):
        if LINE:
            for side, has, count in ((0, has_right, e + 1), (1, has_left, E - e)):
                for n in range(1, E):
                    @pl.when(has & (count == n))
                    def _(side=side, n=n):
                        for p, ref in enumerate((route, xall)):
                            ref = ref.at[pl.ds(0, n)]
                            remote(ref, ref, ag_s.at[side, p], ag_r.at[p, 0], expert=e).wait_send()
        else:
            def drain_line(s, carry):
                for p in range(3):
                    @pl.when((s <= e) & has_right)
                    def _(p=p):
                        gather_to(s, 0, e, (p,))[0].wait_send()

                    @pl.when((s >= e) & has_left)
                    def _(p=p):
                        gather_to(s, 1, e, (p,))[0].wait_send()
                return carry

            lax.fori_loop(0, E, drain_line, 0)
        remote(s1, r1, p_s, p_r.at[0], dp=mate).wait_send()
        remote(s2, r2, q_s, q_r.at[0, 0], dp=mate).wait_send()
        sent = hid.at[:, pl.ds(0, 2 * M - 1)]
        remote(sent, sent, h_s, h_r.at[0, 0], dp=mate).wait_send()

    with jax.named_scope("own"):
        for n in range(2):
            part = pl.ds(n * half, half)
            if LINE:
                total = acc[e, part]
                for at in (jnp.where(mid, 3, 0), jnp.where(mid, 4, 1)):
                    tail(at, e, n, e).wait_recv()
                    total = total + rs_in[at, part].astype(F32)
                out_ref[part] = total.astype(BF16)
            else:
                for at, has in ((e, has_left), (E + e, has_right)):
                    @pl.when(has)
                    def _(at=at):
                        tail(at, e, n, e).wait_recv()
                        acc[e, part] = acc[e, part] + rs_in[at, part].astype(F32)

                out_ref[part] = acc[e, part].astype(BF16)

        if LINE:
            three = rs_s.at[pl.ds(0, E - 1)]
            remote(three, three, t_s, t_r.at[0, 0], expert=e).wait_send()
        else:
            def drain_sums(s, carry):
                @pl.when(s != e)
                def _():
                    for n in range(2):
                        tail(s, s, n, e).wait_send()
                return carry

            lax.fori_loop(0, E, drain_sums, 0)


def on_device(tokens, expert_ids, scores, w_gate, w_up, w_down):
    E, DP = lax.axis_size("expert"), lax.axis_size("dp")
    tok, width = tokens.shape
    top = expert_ids.shape[1]
    EL, _, H = w_gate.shape
    n_exp = E * EL
    CAP = 2 * tok * top // n_exp
    G = min(E, 4)
    NCH = E // G
    LINE = E == 4 and EL == 8
    NB = EL // 2 if LINE else min(3, EL)
    ND = EL // 2 + 2 if LINE else min(3, EL)
    ct = tile_of(width)
    M, hb, R, N = DP // 2, H // DP, G * CAP, EL * NCH
    EP = max(EL, 8)
    NR = EL if LINE else 2 * N
    vmem, dma = pltpu.VMEM, pltpu.SemaphoreType.DMA
    scratch = [
        vmem((NB, width, H), BF16), vmem((NB, width, H), BF16), vmem((ND, H, width), BF16),
        vmem((E, tok, width), BF16), vmem((E, 2 * top, tok), F32),
        vmem((E // 2, EP, 2 * tok), F32), vmem((E // 2, EP, 2 * tok), F32),
        vmem((R, width), BF16),
        vmem((N, M, R, 2 * hb), BF16), vmem((N, M, R, 2 * hb), BF16),
        vmem((N, M, R, 2 * hb), BF16),
        vmem((N, M - 1, R, 2 * hb), BF16), vmem((N, M - 1, R, 2 * hb), BF16),
        vmem((N, DP, R, hb), BF16),
        vmem((E, tok, width), F32),
        vmem((E, tok, width), BF16), vmem((5 if LINE else 2 * E, tok, width), BF16),
        vmem((top, tok), jnp.int32), vmem((top, tok), F32),
        dma((3,)), dma((2, NB)), dma((ND,)), dma((2, 2) if LINE else (2, 3, E)), dma((3, E)),
        dma(()), dma((NR,)), dma(()), dma((NR, M - 1)), dma(()), dma((NR, M - 1)),
        dma((2 * N,)),
        dma(() if LINE else (E, 2)), dma((5 if LINE else 2 * E, 2)),
    ]
    whole = pl.BlockSpec(memory_space=pltpu.VMEM)
    hbm = pl.BlockSpec(memory_space=pl.ANY)
    return pl.pallas_call(
        functools.partial(kernel, (E, DP, EL, NCH, G, CAP, NB, ND, LINE, ct)),
        out_shape=pltpu.VMEM((tok, width), BF16),
        in_specs=[hbm] * 6,
        out_specs=whole,
        scratch_shapes=scratch,
        compiler_params=pltpu.CompilerParams(
            collective_id=0, has_side_effects=True, vmem_limit_bytes=62 * 2**20),
        name="routed_experts",
    )(tokens, expert_ids.T, scores.T, w_gate, w_up, w_down)


def solution(mesh):
    in_specs = (
        P(("groups", "expert"), "dp"),
        P(("groups", "expert"), None),
        P(("groups", "expert"), None),
        P("expert", "dp", None),
        P("expert", "dp", None),
        P("expert", None, "dp"),
    )
    out_specs = P(("groups", "expert"), "dp")
    return jax.shard_map(
        on_device, mesh=mesh, in_specs=in_specs, out_specs=out_specs, check_vma=False
    )
```
